32 devices in a mesh: rows: 16 (over z, y, x), cols: 2 (over core).
Axes of the slice: x: 2, y: 2, z: 4, core: 2. Of those that a mesh axis runs over, the one named last changes fastest.
Arguments:
- row_points: float32 [3, 8192], P(None, 'rows')
- panel_points: bfloat16 [3, 512], P(None, ('rows', 'cols')), may hold values from 0 to 1
- test_vectors: bfloat16 [128, 512], P(None, ('rows', 'cols')), may hold values from -0.25 to 0.25
- leaf_skeleton: int32 [16, 64], P('rows'), may hold values from 0 to 511, as said below
- node_skeleton: int32 [16, 4, 64], P('rows'), may hold values from 0 to 127, as said below
Outputs:
- leaf_interp: float32 [64, 8192], P(None, ('rows', 'cols'))
- transfers: float32 [16, 4, 64, 128], P('rows')
- top_skeleton: float32 [16, 64, 256], P('rows')
The draws below stay inside these ranges and needn't reach their ends.
Inputs may be any that keep to these rules, and one draw needn't show every extreme that they name: `leaf_skeleton`: each leaf's 64 entries are distinct. `node_skeleton`: each entry list holds 64 distinct positions among the 128 stacked rows (the lower child's first); all leaves under the same node have the same list at that level.
All inputs are finite; a program needn't handle non-finite values.
Results may differ from the reference program's by a relative error of at most 0.0049.
Values may be sent and summed in bfloat16 or wider, within the bound.
No kernel may reach another device: no remote copies, remote signals or barrier semaphores. Data moves between devices by JAX's collectives and lax.ppermute only.
A program may use at most 64 MiB of HBM per device.

```python
import jax
import jax.numpy as jnp
from jax import lax

ROWS_DEV = 512
R = 128
K = 64
LEVELS = 4
LEAVES = 16
N = 8192
PANEL = 512


def draw_row_points(key, part):
    leaf_ids = (jnp.arange(N) // ROWS_DEV).astype(jnp.float32)
    jitter = jax.random.uniform(jax.random.fold_in(key, 3), (3, N), jnp.float32)
    along_x = (leaf_ids + jitter[0]) / LEAVES
    return jnp.stack([along_x, jitter[1], jitter[2]])


def leaf_pick(one_key):
    return jax.random.permutation(one_key, ROWS_DEV)[:K]


def node_pick(one_key):
    return jax.random.permutation(one_key, 2 * K)[:K]


def draw_leaf_skeleton(key, part):
    key_list = jax.random.split(jax.random.fold_in(key, 5), LEAVES)
    return jax.vmap(leaf_pick)(key_list).astype(jnp.int32)


def draw_node_skeleton(key, part):
    key_list = jax.random.split(jax.random.fold_in(key, 7), LEVELS * LEAVES)
    node_table = jax.vmap(node_pick)(key_list).reshape(LEVELS, LEAVES, K)
    leaf_ids = jnp.arange(LEAVES)
    row_sets = [node_table[tree_level][jnp.right_shift(leaf_ids, tree_level + 1)] for tree_level in range(LEVELS)]
    return jnp.stack(row_sets, axis=1).astype(jnp.int32)


def shard_levels(rng, extent, cuts, low, high):
    def one(axis_at, blocks):
        draws = jax.random.uniform(jax.random.fold_in(jax.random.fold_in(rng, 6), axis_at), (blocks,), jnp.float32, low / len(cuts), high / len(cuts))
        return jnp.repeat(jnp.exp(draws), extent[axis_at] // blocks).reshape((-1,) + (1,) * (len(extent) - axis_at - 1))

    factor_of = one(*cuts[0])
    for cut in cuts[1:]:
        factor_of = factor_of * one(*cut)
    return factor_of


def bell_draw(rng, dims, width, bound, pieces=(), kind=jnp.bfloat16):
    drawn = width * jax.random.normal(rng, dims, jnp.float32)
    if pieces:
        drawn = drawn * shard_levels(rng, dims, pieces, -0.22, 0.18)
    return jnp.clip(drawn, -bound, bound).astype(kind)


def setup_inputs(seed: int = 0) -> dict:
    streams_of = jax.random.split(jax.random.key(seed), 6)
    return {
        "row_points": draw_row_points(jax.random.fold_in(streams_of[5], 71), 0),
        "panel_points": jnp.clip(1.0 * jax.random.uniform(streams_of[1], (3, PANEL), jnp.float32) ** shard_levels(streams_of[1], (3, PANEL), ((1, 32),), -0.2, 0.2), 0.0, 1.0).astype(jnp.bfloat16),
        "test_vectors": bell_draw(streams_of[2], (R, PANEL), PANEL ** -0.5, 0.25, ((1, 32),)),
        "leaf_skeleton": draw_leaf_skeleton(jax.random.fold_in(streams_of[5], 71), 0),
        "node_skeleton": draw_node_skeleton(jax.random.fold_in(streams_of[5], 71), 0),
    }


KAPPA = 40.0
SMOOTH = 0.05
RIDGE = 0.1
EPSILON = 1e-05

def kernel_block(targets, sources):
    source_f = sources.astype(jnp.float32)
    dist_sq = jnp.zeros((targets.shape[1], source_f.shape[1]), jnp.float32)
    for component in range(3):
        offset = targets[component][:, None] - source_f[component][None, :]
        dist_sq = dist_sq + offset * offset
    radius = jnp.sqrt(dist_sq + SMOOTH * SMOOTH)
    real_part = (jnp.cos(KAPPA * radius) / radius).astype(jnp.bfloat16)
    imag_part = (jnp.sin(KAPPA * radius) / radius).astype(jnp.bfloat16)
    return (real_part, imag_part)

def sample_block(real_part, imag_part, vectors):
    first_half = jnp.dot(real_part.astype(jnp.float32), vectors.T.astype(jnp.float32), preferred_element_type=jnp.float32)
    second_half = jnp.dot(imag_part.astype(jnp.float32), vectors.T.astype(jnp.float32), preferred_element_type=jnp.float32)
    return jnp.concatenate([first_half, second_half], axis=1)

def interpolate(block, skeleton):
    gram_matrix = jnp.dot(skeleton, skeleton.T, precision=lax.Precision.HIGHEST)
    ridge = RIDGE * skeleton.shape[1] * (jnp.mean(skeleton * skeleton) + EPSILON)
    gram_matrix = gram_matrix + ridge * jnp.eye(skeleton.shape[0], dtype=skeleton.dtype)
    factor = jnp.linalg.cholesky(gram_matrix)
    right_side = jnp.dot(skeleton, block.T, precision=lax.Precision.HIGHEST)
    middle = lax.linalg.triangular_solve(factor, right_side, left_side=True, lower=True)
    return lax.linalg.triangular_solve(factor, middle, left_side=True, lower=True, transpose_a=True)

def reference(row_points, panel_points, test_vectors, leaf_skeleton, node_skeleton):

    def leaf_samples(targets):
        real_part, imag_part = kernel_block(targets, panel_points)
        return sample_block(real_part, imag_part, test_vectors)
    blocks = row_points.reshape(3, LEAVES, ROWS_DEV).transpose(1, 0, 2)
    samples = lax.map(leaf_samples, blocks)
    current = jnp.take_along_axis(samples, leaf_skeleton[:, :, None], axis=1)
    leaf_maps = jax.vmap(interpolate)(samples, current)
    leaf_interp = leaf_maps.transpose(1, 0, 2).reshape(K, N)
    level_maps = []
    for tree_level in range(LEVELS):
        nodes = current.shape[0] // 2
        stacked = current.reshape(nodes, 2 * K, current.shape[2])
        chosen = node_skeleton[::2 ** (tree_level + 1), tree_level, :]
        current = jnp.take_along_axis(stacked, chosen[:, :, None], axis=1)
        transfer_maps = jax.vmap(interpolate)(stacked, current)
        level_maps.append(jnp.repeat(transfer_maps, 2 ** (tree_level + 1), axis=0))
    transfers = jnp.stack(level_maps, axis=1)
    top_skeleton = jnp.repeat(current, 2 ** LEVELS, axis=0)
    return (leaf_interp, transfers, top_skeleton)
```

```python
import functools
import math

import jax
import jax.numpy as jnp
from jax import lax
from jax.experimental import pallas as pl
from jax.experimental.pallas import tpu as pltpu
from jax.sharding import PartitionSpec as P

KAPPA = 40.0
SMOOTH = 0.05
RIDGE = 0.1
EPSILON = 1e-05

LANES = 128
SUB = 8
VMEM = pl.BlockSpec(memory_space=pltpu.VMEM)

SIN_POLY = (4.442882834144944, -7.308241154366058, 3.606288956137823, -0.8457635864795654, 0.10920573808065867)
COS_POLY = (1.4142134965650128, -6.978850988238946, 5.739461170681512, -1.8835629873012505, 0.31069819181076774)


def iota(shape, dim):
    return lax.broadcasted_iota(jnp.int32, shape, dim)


def take_lanes(x, index):
    return jnp.take_along_axis(x, index, axis=1)


def swap_halves(x):
    return pltpu.roll(x, LANES // 2, axis=1)


def mm(a, b, dims=((1,), (0,)), precision=None):
    return lax.dot_general(a, b, (dims, ((), ())), precision=precision, preferred_element_type=jnp.float32)


def mm_exact(a, b):
    return mm(a, b, precision=lax.Precision.HIGHEST)


def split3(x):
    high = x.astype(jnp.bfloat16).astype(jnp.float32)
    rest = x - high
    mid = rest.astype(jnp.bfloat16).astype(jnp.float32)
    return high, mid, rest - mid


def pack_kernel(rows_ref, points_ref, vectors_ref, leaf_ref, node_ref, out_ref, stage):
    width = vectors_ref.shape[1]
    half = LANES // 2
    low = iota((1, LANES), 1) < half
    stage[...] = jnp.zeros_like(stage)
    stage[0:1, 0:half] = leaf_ref[...].astype(jnp.float32)
    stage[1:5, 0:half] = node_ref[0].astype(jnp.float32)
    stage[5:8, 0:width] = points_ref[...].astype(jnp.float32)
    s = stage[...]
    index = s[0:1]
    index = (index + swap_halves(jnp.broadcast_to(index, (SUB, LANES)))[0:1]).astype(jnp.int32)
    index = jnp.broadcast_to(index, (SUB, LANES))
    stage[0:3, :] = rows_ref[:, 0:LANES]
    found = jnp.zeros((SUB, LANES), jnp.float32)
    for tile in range(rows_ref.shape[1] // LANES):
        stage[0:3, :] = rows_ref[:, tile * LANES : (tile + 1) * LANES]
        picked = take_lanes(stage[...], index & (LANES - 1))
        found = jnp.where(index // LANES == tile, picked, found)
    high, mid, tail = split3(found)
    swapped = swap_halves(s)
    lines = [
        jnp.where(low, high[0:1], mid[0:1]),
        jnp.where(low, tail[0:1], high[1:2]),
        jnp.where(low, mid[1:2], tail[1:2]),
        jnp.where(low, high[2:3], mid[2:3]),
        tail[2:3],
        jnp.where(low, s[1:2], swapped[2:3]),
        jnp.where(low, s[3:4], swapped[4:5]),
        s[5:6] + pltpu.roll(s, width, axis=1)[6:7] + pltpu.roll(s, 2 * width, axis=1)[7:8],
    ]
    eye = (iota((width, width), 0) == iota((width, width), 1)).astype(jnp.bfloat16)
    columns = mm(eye, vectors_ref[...], dims=((1,), (1,)))
    block = jnp.concatenate([columns] + lines, axis=0).astype(jnp.bfloat16)

    def put(device, unused):
        out_ref[device] = block
        return unused

    lax.fori_loop(0, out_ref.shape[0], put, 0)


def main_kernel(levels, got_ref, rows_ref, node_ref, interp_ref, maps_ref, top_ref, stage, kre_ref, kim_ref, samples_ref):
    half = LANES // 2
    leaf = lax.axis_index("rows")
    column = lax.axis_index("cols")
    cols = lax.axis_size("cols")
    group_leaves = 2**levels
    group_devices = group_leaves * cols
    devices = got_ref.shape[0]
    width = got_ref.shape[1] - SUB
    lane8 = iota((SUB, LANES), 1)
    sub8 = iota((SUB, LANES), 0)
    low8 = lane8 < half
    member = leaf % group_leaves
    mine = sub8 == member // 2

    group_start = (leaf // group_leaves) * group_devices
    extra = got_ref[pl.ds(group_start, group_devices), width : width + SUB, :].astype(jnp.float32)
    extra = extra.reshape(group_devices * SUB, LANES).astype(jnp.bfloat16)
    shape = (7 * 16, group_devices * SUB)
    at = iota(shape, 0)
    source = ((at % 8) * 2 + (at // 8) % 2) * (cols * SUB) + at // 16
    picked = mm((iota(shape, 1) == source).astype(jnp.bfloat16), extra)
    even = [picked[r * 16 : r * 16 + 8] for r in range(7)]
    odd = [picked[r * 16 + 8 : r * 16 + 16] for r in range(7)]
    even_s = [swap_halves(v) for v in even]
    odd_s = [swap_halves(v) for v in odd]
    coords = [
        jnp.where(low8, even[0] + even_s[0] + even[1], odd[0] + odd_s[0] + odd_s[1]),
        jnp.where(low8, even_s[1] + (even[2] + even_s[2]), odd[1] + (odd[2] + odd_s[2])),
        jnp.where(low8, even[3] + even_s[3] + even[4], odd[3] + odd_s[3] + odd[4]),
    ]
    lists = [
        jnp.where(low8, even[5], even_s[5]).astype(jnp.int32),
        jnp.where(low8, even_s[5], even[5]).astype(jnp.int32),
        jnp.where(low8, even[6], even_s[6]).astype(jnp.int32),
        jnp.where(low8, even_s[6], even[6]).astype(jnp.int32),
    ]

    def own_row(x):
        return jnp.sum(jnp.where(mine, x, jnp.zeros_like(x)), axis=0, keepdims=True)

    siblings = []
    own_lists = [own_row(lists[0])]
    stacked = coords
    for level in range(1, levels):
        own = [take_lanes(v, lists[level - 1]) for v in stacked]
        step = 2 ** (level - 1)
        upper = (sub8 // step) % 2 == 1
        other = [jnp.where(upper, pltpu.roll(v, step, axis=0), pltpu.roll(v, SUB - step, axis=0)) for v in own]
        siblings.append([own_row(v) for v in other])
        stacked = [jnp.where(low8 == upper, b, a) for a, b in zip(own, other)]
        own_lists.append(own_row(lists[level]))
    low1 = iota((1, LANES), 1) < half
    tiles = [[own_row(v) for v in coords]]
    tiles.append([jnp.where(low1, a, b) for a, b in zip(siblings[0], siblings[1])])
    tiles.append(siblings[2])
    own_rows = rows_ref.shape[1] // cols
    own_tiles = own_rows // LANES
    start = pl.multiple_of(column * own_rows, LANES)
    own_points = rows_ref[:, pl.ds(start, own_rows)]
    for tile in range(own_tiles):
        part = own_points[:, tile * LANES : (tile + 1) * LANES]
        tiles.append([part[c : c + 1] for c in range(3)])
    total = len(tiles) * LANES

    block_devices = min(devices, group_devices)
    block = block_devices * width
    vec_count = got_ref.shape[2]
    eye = (iota((vec_count, vec_count), 0) == iota((vec_count, vec_count), 1)).astype(jnp.bfloat16)
    shape = (block, block_devices * SUB)
    spread = (iota(shape, 1) == (iota(shape, 0) // width) * SUB + SUB - 1).astype(jnp.bfloat16)
    shape = (block, LANES)
    keep = ((iota(shape, 1) % width) == (iota(shape, 0) % width)) & (iota(shape, 1) < 3 * width)
    shape = (LANES, 3 * LANES)
    collect = (iota(shape, 0) // width == iota(shape, 1) // LANES).astype(jnp.bfloat16)

    def panel_block(number, first):
        got = got_ref[pl.ds(number * block_devices, block_devices)].astype(jnp.float32)
        vectors = got[:, 0:width, :].reshape(block, vec_count).astype(jnp.bfloat16)
        tail = got[:, width : width + SUB, :].reshape(block_devices * SUB, LANES).astype(jnp.bfloat16)
        points = mm(spread, tail)
        points = jnp.where(keep, points, 0.0).astype(jnp.bfloat16)
        points = mm(points, collect)
        stage_p = [points[:, c * LANES : (c + 1) * LANES] for c in range(3)]
        for tile, target in enumerate(tiles):
            for at in range(0, block, 16):
                dist = jnp.full((16, LANES), SMOOTH * SMOOTH, jnp.float32)
                for c in range(3):
                    offset = target[c] - stage_p[c][at : at + 16]
                    dist = dist + offset * offset
                inverse = lax.rsqrt(dist)
                turns = (dist * inverse) * (KAPPA / (2 * math.pi))
                f = turns - jnp.round(turns)
                u = f * f
                sine = SIN_POLY[4]
                cosine = COS_POLY[4]
                for degree in (3, 2, 1, 0):
                    sine = sine * u + SIN_POLY[degree]
                    cosine = cosine * u + COS_POLY[degree]
                sine = sine * f
                real = (1.0 - sine * sine) * inverse
                imag = (sine * cosine) * inverse
                kre_ref[at : at + 16, tile * LANES : (tile + 1) * LANES] = real.astype(jnp.bfloat16)
                kim_ref[at : at + 16, tile * LANES : (tile + 1) * LANES] = imag.astype(jnp.bfloat16)
        vectors = mm(eye, vectors, dims=((1,), (1,))).astype(jnp.bfloat16)
        new_re = mm(vectors, kre_ref[...])
        new_im = mm(vectors, kim_ref[...])
        if first:
            samples_ref[0:vec_count, :] = new_re
            samples_ref[vec_count : 2 * vec_count, :] = new_im
        else:
            samples_ref[0:vec_count, :] += new_re
            samples_ref[vec_count : 2 * vec_count, :] += new_im

    panel_block(0, True)
    if devices > block_devices:

        def more(number, unused):
            panel_block(number, False)
            return unused

        lax.fori_loop(1, devices // block_devices, more, 0)

    full = (2 * vec_count, LANES)
    low = iota(full, 1) < half
    pair0 = samples_ref[:, 0:LANES]
    pair12 = samples_ref[:, LANES : 2 * LANES]
    pair12_s = swap_halves(pair12)
    pair3 = samples_ref[:, 2 * LANES : 3 * LANES]

    def is_upper(level):
        return ((iota(full, 0) * 0 + member) // 2**level) % 2 == 1

    stacks = [pair0]
    skels = [jnp.where(is_upper(0) == low, swap_halves(pair0), pair0)]
    skels_full = []
    for level in range(levels):
        picked = take_lanes(stacks[level], jnp.broadcast_to(own_lists[level], full))
        skels_full.append(picked)
        if level + 1 < levels:
            up = is_upper(level + 1)
            if level == 0:
                other = jnp.where(up, pair12, pair12_s)
            elif level == 1:
                other = jnp.where(up, pair12_s, pair12)
            else:
                other = pair3
            stacks.append(jnp.where(low == up, other, picked))
    own0 = jnp.where(is_upper(0), swap_halves(pair0), pair0)
    own0 = jnp.where(low, own0, swap_halves(own0))
    skels = [own0] + skels_full

    def rows_of(a, b):
        return jnp.where(low, a, b).T

    two = [rows_of(skels[0], skels[1]), rows_of(skels[2], skels[3]), rows_of(skels[4], skels[4])]
    row_form = [two[0][0:half], two[0][half:], two[1][0:half], two[1][half:], two[2][0:half]]
    top_ref[0] = row_form[4]

    right_leaf = mm_exact(row_form[0], samples_ref[:, 3 * LANES : (3 + own_tiles) * LANES])
    right_maps = [mm_exact(row_form[level + 1], stacks[level]) for level in range(levels)]
    square = (half, LANES)
    low64 = iota(square, 1) < half
    grams = [mm_exact(row_form[0], skels[0])]
    for level in range(levels):
        grams.append(take_lanes(right_maps[level], jnp.broadcast_to(own_lists[level], square)))
    pairs = []
    diagonal = iota(square, 0) == iota(square, 1) % half
    for a, b in ((0, 1), (2, 3), (4, 4)):
        gram = jnp.where(low64, grams[a], grams[b])
        trace = jnp.sum(jnp.where(diagonal, gram, 0.0), axis=0, keepdims=True)
        first = jnp.sum(jnp.where(low1, trace, 0.0), axis=1, keepdims=True)
        second = jnp.sum(jnp.where(low1, 0.0, trace), axis=1, keepdims=True)
        trace = jnp.where(low1, first, second)
        ridge = RIDGE * (2 * vec_count) * (trace * (1.0 / (half * 2 * vec_count)) + EPSILON)
        gram = gram + jnp.where(diagonal, ridge, 0.0)
        pairs.append([gram[r * SUB : (r + 1) * SUB] for r in range(half // SUB)])

    where_in_half = lane8 % half
    half_base = lane8 - where_in_half

    def eliminate(turn, blocks):
        out = [list(b) for b in blocks]
        for s in range(SUB):
            pivot_at = turn * SUB + s
            index = half_base + pivot_at
            here = where_in_half == pivot_at
            for n in range(len(out)):
                a = out[n]
                column_of = [take_lanes(v, index) for v in a]
                pivot = jnp.broadcast_to(column_of[0][s : s + 1], (SUB, LANES))
                line = jnp.broadcast_to(a[0][s : s + 1], (SUB, LANES))
                line = jnp.where(here, 1.0, line) * (1.0 / pivot)
                a = [jnp.where(here, 0.0, v) - c * line for v, c in zip(a, column_of)]
                a[0] = jnp.where(sub8 == s, line, a[0])
                out[n] = a
        return tuple(tuple(b[1:] + b[:1]) for b in out)

    done = lax.fori_loop(0, half // SUB, eliminate, tuple(tuple(b) for b in pairs))
    inverse = [jnp.concatenate(list(b), axis=0) for b in done]

    zero = jnp.zeros((half, LANES), jnp.float32)
    wide = jnp.zeros((half, own_rows), jnp.float32)
    result = mm_exact(
        inverse[0],
        jnp.concatenate(
            [jnp.concatenate([right_leaf, zero], axis=1), jnp.concatenate([wide, right_maps[0]], axis=1)], axis=0
        ),
    )
    interp_ref[...] = result[:, 0:own_rows]
    maps_ref[0, 0] = result[:, own_rows:]
    result = mm_exact(
        inverse[1],
        jnp.concatenate(
            [jnp.concatenate([right_maps[1], zero], axis=1), jnp.concatenate([zero, right_maps[2]], axis=1)], axis=0
        ),
    )
    maps_ref[0, 1] = result[:, 0:LANES]
    maps_ref[0, 2] = result[:, LANES:]
    maps_ref[0, 3] = mm_exact(inverse[2], jnp.concatenate([right_maps[3], zero], axis=0))


def body(row_points, panel_points, test_vectors, leaf_skeleton, node_skeleton):
    devices = lax.axis_size("rows") * lax.axis_size("cols")
    vec_count, width = test_vectors.shape
    rows_here = row_points.shape[1]
    levels, skel = node_skeleton.shape[1:]
    packed = pl.pallas_call(
        pack_kernel,
        out_shape=jax.ShapeDtypeStruct((devices, width + SUB, vec_count), jnp.bfloat16),
        in_specs=[VMEM] * 5,
        out_specs=VMEM,
        scratch_shapes=[pltpu.VMEM((SUB, LANES), jnp.float32)],
    )(row_points, panel_points, test_vectors, leaf_skeleton, node_skeleton)
    got = lax.all_to_all(packed, ("rows", "cols"), 0, 0, tiled=True)
    own_rows = rows_here // lax.axis_size("cols")
    lanes = 3 * LANES + own_rows
    block = min(devices, 2**levels * lax.axis_size("cols")) * width
    return pl.pallas_call(
        functools.partial(main_kernel, levels),
        out_shape=(
            jax.ShapeDtypeStruct((skel, own_rows), jnp.float32),
            jax.ShapeDtypeStruct((1, levels, skel, 2 * skel), jnp.float32),
            jax.ShapeDtypeStruct((1, skel, 2 * vec_count), jnp.float32),
        ),
        in_specs=[VMEM] * 3,
        out_specs=(VMEM, VMEM, VMEM),
        scratch_shapes=[
            pltpu.VMEM((SUB, LANES), jnp.float32),
            pltpu.VMEM((block, lanes), jnp.bfloat16),
            pltpu.VMEM((block, lanes), jnp.bfloat16),
            pltpu.VMEM((2 * vec_count, lanes), jnp.float32),
        ],
    )(got, row_points, node_skeleton)


def solution(mesh):
    placed = (
        P(None, "rows"),
        P(None, ("rows", "cols")),
        P(None, ("rows", "cols")),
        P("rows", None),
        P("rows", None, None),
    )
    return jax.shard_map(
        body,
        mesh=mesh,
        in_specs=placed,
        out_specs=(P(None, ("rows", "cols")), P("rows", None, None, None), P("rows", None, None)),
        check_vma=False,
    )
```

```python
import functools
import math

import jax
import jax.numpy as jnp
import numpy as np
from jax import lax
from jax.experimental import pallas as pl
from jax.experimental.pallas import tpu as pltpu
from jax.sharding import PartitionSpec as P

KAPPA = 40.0
SMOOTH = 0.05
RIDGE = 0.1
EPSILON = 1e-05

LANES = 128
SUB = 8
VMEM = pl.BlockSpec(memory_space=pltpu.VMEM)

TURNS = KAPPA / (2 * math.pi)
SIN_POLY = (4.442867902871973, -7.30744341774541, 3.594788055359915, -0.7843739844598376)
COS_POLY = (1.4142134965650128, -6.978850988238946, 5.739461170681512, -1.8835629873012505, 0.31069819181076774)


def bf16_parts(value):
    parts = []
    for unused in range(3):
        parts.append(float(np.float32(value).astype(jnp.bfloat16)))
        value -= parts[-1]
    return parts


SCALE_PARTS = bf16_parts(TURNS * TURNS)


def iota(shape, dim):
    return lax.broadcasted_iota(jnp.int32, shape, dim)


def take_lanes(x, index):
    return jnp.take_along_axis(x, index, axis=1)


def swap_halves(x):
    return pltpu.roll(x, LANES // 2, axis=1)


def mm(a, b, dims=((1,), (0,)), precision=None):
    return lax.dot_general(a, b, (dims, ((), ())), precision=precision, preferred_element_type=jnp.float32)


def split2(x):
    high = x.astype(jnp.bfloat16)
    return high, (x - high.astype(jnp.float32)).astype(jnp.bfloat16)


def mm_split(a, b):
    (a_high, a_low), (b_high, b_low) = a, b
    return mm(jnp.concatenate([a_high, a_high, a_low], axis=1), jnp.concatenate([b_high, b_low, b_high], axis=0))


def split3(x):
    high = x.astype(jnp.bfloat16).astype(jnp.float32)
    rest = x - high
    mid = rest.astype(jnp.bfloat16).astype(jnp.float32)
    return high, mid, rest - mid


def pack_kernel(rows_ref, points_ref, vectors_ref, leaf_ref, node_ref, out_ref, stage):
    width = vectors_ref.shape[0]
    half = LANES // 2
    low = iota((1, LANES), 1) < half
    stage[...] = jnp.zeros_like(stage)
    stage[0:1, 0:half] = leaf_ref[...].astype(jnp.float32)
    stage[1:5, 0:half] = node_ref[0].astype(jnp.float32)
    stage[5:8, 0:width] = points_ref[...].astype(jnp.float32)
    s = stage[...]
    index = s[0:1]
    index = (index + swap_halves(jnp.broadcast_to(index, (SUB, LANES)))[0:1]).astype(jnp.int32)
    index = jnp.broadcast_to(index, (SUB, LANES))
    stage[0:3, :] = rows_ref[:, 0:LANES]
    found = jnp.zeros((SUB, LANES), jnp.float32)
    for tile in range(rows_ref.shape[1] // LANES):
        stage[0:3, :] = rows_ref[:, tile * LANES : (tile + 1) * LANES]
        picked = take_lanes(stage[...], index & (LANES - 1))
        found = jnp.where(index // LANES == tile, picked, found)
    high, mid, tail = split3(found)
    swapped = swap_halves(s)
    lines = [
        jnp.where(low, high[0:1], mid[0:1]),
        jnp.where(low, tail[0:1], high[1:2]),
        jnp.where(low, mid[1:2], tail[1:2]),
        jnp.where(low, high[2:3], mid[2:3]),
        tail[2:3],
        jnp.where(low, s[1:2], swapped[2:3]),
        jnp.where(low, s[3:4], swapped[4:5]),
        s[5:6] + pltpu.roll(s, width, axis=1)[6:7] + pltpu.roll(s, 2 * width, axis=1)[7:8],
    ]
    block = jnp.concatenate([vectors_ref[...].astype(jnp.float32)] + lines, axis=0).astype(jnp.bfloat16)

    def put(device, unused):
        out_ref[device] = block
        return unused

    lax.fori_loop(0, out_ref.shape[0], put, 0)


def evaluate(dist):
    inverse = lax.rsqrt(dist)
    turns = dist * inverse
    f = turns - jnp.round(turns)
    u = f * f
    scale = math.sqrt(TURNS)
    sine = SIN_POLY[-1] * scale
    cosine = COS_POLY[-1] * scale
    for value in SIN_POLY[-2::-1]:
        sine = sine * u + value * scale
    for value in COS_POLY[-2::-1]:
        cosine = cosine * u + value * scale
    sine = sine * f
    real = (TURNS - sine * sine) * inverse
    imag = (sine * cosine) * inverse
    return real.astype(jnp.bfloat16), imag.astype(jnp.bfloat16)


def main_kernel(levels, got_ref, rows_ref, interp_ref, maps_ref, top_ref, left_ref, kre_ref, kim_ref, samples_ref):
    half = LANES // 2
    leaf = lax.axis_index("rows")
    column = lax.axis_index("cols")
    cols = lax.axis_size("cols")
    group_leaves = 2**levels
    group_devices = group_leaves * cols
    devices = got_ref.shape[0]
    width = got_ref.shape[1] - SUB
    width_bits = width.bit_length() - 1
    lane8 = iota((SUB, LANES), 1)
    sub8 = iota((SUB, LANES), 0)
    low8 = lane8 < half
    member = leaf & (group_leaves - 1)
    mine = sub8 == member >> 1

    group_start = (leaf // group_leaves) * group_devices
    extra = got_ref[pl.ds(group_start, group_devices), width : width + SUB, :].astype(jnp.float32)
    extra = extra.reshape(group_devices * SUB, LANES).astype(jnp.bfloat16)
    shape = (7 * 16, group_devices * SUB)
    at = iota(shape, 0)
    source = ((at & 7) * 2 + ((at >> 3) & 1)) * (cols * SUB) + (at >> 4)
    picked = mm((iota(shape, 1) == source).astype(jnp.bfloat16), extra)
    even = [picked[r * 16 : r * 16 + 8] for r in range(7)]
    odd = [picked[r * 16 + 8 : r * 16 + 16] for r in range(7)]
    even_s = [swap_halves(v) for v in even]
    odd_s = [swap_halves(v) for v in odd]
    coords = [
        jnp.where(low8, even[0] + even_s[0] + even[1], odd[0] + odd_s[0] + odd_s[1]),
        jnp.where(low8, even_s[1] + (even[2] + even_s[2]), odd[1] + (odd[2] + odd_s[2])),
        jnp.where(low8, even[3] + even_s[3] + even[4], odd[3] + odd_s[3] + odd[4]),
    ]
    lists = [
        jnp.where(low8, even[5], even_s[5]).astype(jnp.int32),
        jnp.where(low8, even_s[5], even[5]).astype(jnp.int32),
        jnp.where(low8, even[6], even_s[6]).astype(jnp.int32),
        jnp.where(low8, even_s[6], even[6]).astype(jnp.int32),
    ]

    def own_row(x):
        return jnp.sum(jnp.where(mine, x, jnp.zeros_like(x)), axis=0, keepdims=True)

    siblings = []
    own_lists = [own_row(lists[0])]
    stacked = coords
    for level in range(1, levels):
        own = [take_lanes(v, lists[level - 1]) for v in stacked]
        step = 2 ** (level - 1)
        upper = (sub8 & step) != 0
        other = [jnp.where(upper, pltpu.roll(v, step, axis=0), pltpu.roll(v, SUB - step, axis=0)) for v in own]
        siblings.append([own_row(v) for v in other])
        stacked = [jnp.where(low8 == upper, b, a) for a, b in zip(own, other)]
        own_lists.append(own_row(lists[level]))
    low1 = iota((1, LANES), 1) < half
    tiles = [[own_row(v) for v in coords]]
    tiles.append([jnp.where(low1, a, b) for a, b in zip(siblings[0], siblings[1])])
    tiles.append(siblings[2])
    tree_lanes = len(tiles) * LANES
    own_rows = rows_ref.shape[1] // cols
    start = pl.multiple_of(column * own_rows, LANES)
    own_points = rows_ref[:, pl.ds(start, own_rows)]

    def right_side(points):
        lanes = points[0].shape[1]
        lines = []
        norm = jnp.full((1, lanes), SMOOTH * SMOOTH, jnp.float32)
        for x in points:
            norm = norm + x * x
            lines += split3(x * (-2 * TURNS * TURNS))
        for repeat in range(6):
            lines += [jnp.full((1, lanes), v, jnp.float32) for v in SCALE_PARTS]
        lines += split3(norm * (TURNS * TURNS))
        lines.append(jnp.zeros((LANES - len(lines), lanes), jnp.float32))
        return jnp.concatenate(lines, axis=0).astype(jnp.bfloat16)

    right_tree = jnp.concatenate([right_side(t) for t in tiles], axis=1)
    right_own = right_side([own_points[c : c + 1] for c in range(3)])

    block_devices = min(devices, group_devices)
    single = block_devices == devices
    block = block_devices * width
    vec_count = got_ref.shape[2]
    eye = (iota((vec_count, vec_count), 0) == iota((vec_count, vec_count), 1)).astype(jnp.bfloat16)
    shape = (block, block_devices * SUB)
    spread = (iota(shape, 1) == ((iota(shape, 0) >> width_bits) * SUB + SUB - 1)).astype(jnp.bfloat16)
    shape = (block, LANES)
    lane_of = iota(shape, 1)
    keep = (((lane_of ^ iota(shape, 0)) & (width - 1)) == 0) & (lane_of < 3 * width)
    ones = ((lane_of >= 27) & (lane_of < 30)).astype(jnp.bfloat16)
    shape = (LANES, LANES)
    away = iota(shape, 1) - 3 * (iota(shape, 0) >> width_bits)
    within = iota(shape, 0) < 3 * width
    collect = jnp.concatenate(
        [(within & (away >= first) & (away < first + 3)).astype(jnp.bfloat16) for first in (0, 9, 18)], axis=0
    )

    def panel_vectors(number):
        got = got_ref[pl.ds(number * block_devices, block_devices), 0:width, :].astype(jnp.float32)
        vectors = got.reshape(block, vec_count).astype(jnp.bfloat16)
        return mm(eye, vectors, dims=((1,), (1,))).astype(jnp.bfloat16)

    def panel_left(number):
        tail = got_ref[pl.ds(number * block_devices, block_devices), width : width + SUB, :].astype(jnp.float32)
        tail = tail.reshape(block_devices * SUB, LANES).astype(jnp.bfloat16)
        points = jnp.where(keep, mm(spread, tail), 0.0)
        high, low = split2(points * points)
        left_ref[...] = mm(jnp.concatenate([points.astype(jnp.bfloat16), high, low], axis=1), collect).astype(jnp.bfloat16) + ones

    def fill(at, count, right, lane):
        dist = mm(left_ref[pl.ds(at, count), :], right)
        lanes = right.shape[1]
        kre_ref[pl.ds(at, count), lane : lane + lanes], kim_ref[pl.ds(at, count), lane : lane + lanes] = evaluate(dist)

    def sample(vectors, lane, lanes):
        both = [mm(vectors, k[:, lane : lane + lanes]) for k in (kre_ref, kim_ref)]
        return jnp.concatenate(both, axis=0)

    chunk = min(LANES, block)
    panel_left(0)
    vectors = panel_vectors(0)
    for at in range(0, block, chunk):
        fill(at, chunk, right_tree, 0)
    samples_ref[:, 0:tree_lanes] = sample(vectors, 0, tree_lanes)
    if not single:
        for at in range(0, block, chunk):
            fill(at, chunk, right_own, tree_lanes)
        samples_ref[:, tree_lanes:] = sample(vectors, tree_lanes, own_rows)

        def more(number, unused):
            panel_left(number)
            for at in range(0, block, chunk):
                fill(at, chunk, right_tree, 0)
                fill(at, chunk, right_own, tree_lanes)
            samples_ref[...] += sample(panel_vectors(number), 0, tree_lanes + own_rows)
            return unused

        lax.fori_loop(1, devices // block_devices, more, 0)

    full = (2 * vec_count, LANES)
    low = iota(full, 1) < half
    pair0 = samples_ref[:, 0:LANES]
    pair0_s = swap_halves(pair0)
    pair12 = samples_ref[:, LANES : 2 * LANES]
    pair12_s = swap_halves(pair12)
    pair3 = samples_ref[:, 2 * LANES : 3 * LANES]

    def is_upper(level, shape):
        return (jnp.full(shape, member, jnp.int32) & 2**level) != 0

    upper0 = is_upper(0, full)
    stacks = [pair0]
    skels = [jnp.where(upper0 == low, pair0_s, pair0)]
    for level in range(levels):
        picked = take_lanes(stacks[level], jnp.broadcast_to(own_lists[level], full))
        skels.append(picked)
        if level + 1 < levels:
            up = is_upper(level + 1, full)
            if level == 0:
                other = jnp.where(up, pair12, pair12_s)
            elif level == 1:
                other = jnp.where(up, pair12_s, pair12)
            else:
                other = pair3
            stacks.append(jnp.where(low == up, other, picked))

    two = [jnp.where(low, skels[0], skels[1]).T, jnp.where(low, skels[2], skels[3]).T, skels[4].T]
    row_form = [two[0][0:half], two[0][half:], two[1][0:half], two[1][half:], two[2][0:half]]
    top_ref[0] = row_form[4]
    row_form = [split2(v) for v in row_form]

    stacks = [split2(v) for v in stacks]
    square = (half, LANES)
    low64 = iota(square, 1) < half
    right_maps = [mm_split(row_form[level + 1], stacks[level]) for level in range(levels)]
    gram = mm_split(row_form[0], stacks[0])
    grams = [jnp.where(is_upper(0, square) == low64, swap_halves(gram), gram)]
    for level in range(levels):
        grams.append(take_lanes(right_maps[level], jnp.broadcast_to(own_lists[level], square)))
    pairs = []
    diagonal = iota(square, 0) == (iota(square, 1) & (half - 1))
    for a, b in ((0, 1), (2, 3), (4, 4)):
        gram = jnp.where(low64, grams[a], grams[b])
        trace = jnp.sum(jnp.where(diagonal, gram, 0.0), axis=0, keepdims=True)
        first = jnp.sum(jnp.where(low1, trace, 0.0), axis=1, keepdims=True)
        second = jnp.sum(jnp.where(low1, 0.0, trace), axis=1, keepdims=True)
        trace = jnp.where(low1, first, second)
        ridge = RIDGE * (2 * vec_count) * (trace * (1.0 / (half * 2 * vec_count)) + EPSILON)
        gram = gram + jnp.where(diagonal, ridge, 0.0)
        pairs.append([gram[r * SUB : (r + 1) * SUB] for r in range(half // SUB)])

    where_in_half = lane8 & (half - 1)
    half_base = lane8 - where_in_half
    blocks = half // SUB
    piece = block // blocks

    def spread_row(x, row):
        return jnp.broadcast_to(x[row : row + 1], (SUB, LANES))

    zero8 = jnp.zeros((SUB, LANES), jnp.float32)
    for turn in range(blocks):
        first = turn * SUB
        ahead = turn + 1 if turn + 1 < blocks else None
        within_turn = (where_in_half >> 3) == turn
        diagonals = [[take_lanes(a[turn], half_base + (first + j)) for j in range(SUB)] for a in pairs]
        if ahead is not None:
            nexts = [[take_lanes(a[ahead], half_base + (first + j)) for j in range(SUB)] for a in pairs]
        lines = [a[turn] for a in pairs]
        for s in range(SUB):
            if single and s % 2 == 0:
                fill(turn * piece + s // 2 * (piece // 4), piece // 4, right_own, tree_lanes)
            here = where_in_half == first + s
            row = sub8 == s
            for n in range(len(pairs)):
                columns = diagonals[n]
                inverse = 1.0 / spread_row(columns[s], s)
                column = jnp.where(row, -1.0, columns[s])
                line = jnp.where(here, 1.0, spread_row(lines[n], s)) * inverse
                lines[n] = jnp.where(here | row, 0.0, lines[n]) - column * line
                for j in range(s + 1, SUB):
                    factor = spread_row(columns[j], s) * inverse
                    columns[j] = jnp.where(row, 0.0, columns[j]) - column * factor
        for n, a in enumerate(pairs):
            line = lines[n]
            cleared = [jnp.where(within_turn, 0.0, v) for v in a]
            others = [b for b in range(blocks) if b not in (turn, ahead)]
            if ahead is not None:
                terms = [nexts[n][j] * spread_row(line, j) for j in range(SUB)]
                while len(terms) > 1:
                    terms = [x + y for x, y in zip(terms[::2], terms[1::2])]
            stacked = [zero8] * (2 * blocks)
            stacked[turn] = jnp.where(low8, line, 0.0)
            stacked[blocks + turn] = jnp.where(low8, 0.0, line)
            left = split2(jnp.concatenate([a[b] for b in others], axis=0))
            product = mm_split(left, split2(jnp.concatenate(stacked, axis=0)))
            for number, b in enumerate(others):
                a[b] = cleared[b] - product[number * SUB : (number + 1) * SUB]
            if ahead is not None:
                a[ahead] = cleared[ahead] - terms[0]
            a[turn] = line

    inverses = []
    for a in pairs:
        both = jnp.concatenate(a, axis=0)
        inverses.append(split2(jnp.concatenate([jnp.where(low64, both, 0.0), jnp.where(low64, 0.0, both)], axis=0)))
    if single:
        own_samples = sample(vectors, tree_lanes, own_rows)
    else:
        own_samples = samples_ref[:, tree_lanes:]
    right_leaf = mm_split(row_form[0], split2(own_samples))

    def rows_from(pair, first, last):
        return pair[0][first:last], pair[1][first:last]

    result = mm_split(inverses[1], split2(jnp.concatenate([right_maps[1], right_maps[2]], axis=0)))
    maps_ref[0, 1] = result[0:half]
    maps_ref[0, 2] = result[half:]
    zero = jnp.zeros((half, LANES), jnp.float32)
    maps_ref[0, 3] = mm_split(rows_from(inverses[2], 0, half), split2(jnp.concatenate([right_maps[3], zero], axis=0)))
    maps_ref[0, 0] = mm_split(rows_from(inverses[0], half, LANES), split2(jnp.concatenate([zero, right_maps[0]], axis=0)))
    zero = jnp.zeros((half, own_rows), jnp.float32)
    interp_ref[...] = mm_split(rows_from(inverses[0], 0, half), split2(jnp.concatenate([right_leaf, zero], axis=0)))


def body(row_points, panel_points, test_vectors, leaf_skeleton, node_skeleton):
    devices = lax.axis_size("rows") * lax.axis_size("cols")
    vec_count, width = test_vectors.shape
    rows_here = row_points.shape[1]
    levels, skel = node_skeleton.shape[1:]
    packed = pl.pallas_call(
        pack_kernel,
        out_shape=jax.ShapeDtypeStruct((devices, width + SUB, vec_count), jnp.bfloat16),
        in_specs=[VMEM] * 5,
        out_specs=VMEM,
        scratch_shapes=[pltpu.VMEM((SUB, LANES), jnp.float32)],
    )(row_points, panel_points, test_vectors.T, leaf_skeleton, node_skeleton)
    got = lax.all_to_all(packed, ("rows", "cols"), 0, 0, tiled=True)
    own_rows = rows_here // lax.axis_size("cols")
    lanes = 3 * LANES + own_rows
    block = min(devices, 2**levels * lax.axis_size("cols")) * width
    return pl.pallas_call(
        functools.partial(main_kernel, levels),
        out_shape=(
            jax.ShapeDtypeStruct((skel, own_rows), jnp.float32),
            jax.ShapeDtypeStruct((1, levels, skel, 2 * skel), jnp.float32),
            jax.ShapeDtypeStruct((1, skel, 2 * vec_count), jnp.float32),
        ),
        in_specs=[VMEM] * 2,
        out_specs=(VMEM, VMEM, VMEM),
        scratch_shapes=[
            pltpu.VMEM((block, LANES), jnp.bfloat16),
            pltpu.VMEM((block, lanes), jnp.bfloat16),
            pltpu.VMEM((block, lanes), jnp.bfloat16),
            pltpu.VMEM((2 * vec_count, lanes), jnp.float32),
        ],
    )(got, row_points)


def solution(mesh):
    placed = (
        P(None, "rows"),
        P(None, ("rows", "cols")),
        P(None, ("rows", "cols")),
        P("rows", None),
        P("rows", None, None),
    )
    return jax.shard_map(
        body,
        mesh=mesh,
        in_specs=placed,
        out_specs=(P(None, ("rows", "cols")), P("rows", None, None, None), P("rows", None, None)),
        check_vma=False,
    )
```

```python
import functools
import math

import jax
import jax.numpy as jnp
import numpy as np
from jax import lax
from jax.experimental import pallas as pl
from jax.experimental.pallas import tpu as pltpu
from jax.sharding import PartitionSpec as P

KAPPA = 40.0
SMOOTH = 0.05
RIDGE = 0.1
EPSILON = 1e-05

LANES = 128
SUB = 8
VMEM = pl.BlockSpec(memory_space=pltpu.VMEM)

TURNS = KAPPA / (2 * math.pi)
SIN_POLY = (4.442867902871973, -7.30744341774541, 3.594788055359915, -0.7843739844598376)
COS_POLY = (1.4142134965650128, -6.978850988238946, 5.739461170681512, -1.8835629873012505, 0.31069819181076774)


def bf16_parts(value):
    parts = []
    for unused in range(3):
        parts.append(float(np.float32(value).astype(jnp.bfloat16)))
        value -= parts[-1]
    return parts


SCALE_PARTS = bf16_parts(TURNS * TURNS)


def iota(shape, dim):
    return lax.broadcasted_iota(jnp.int32, shape, dim)


def take_lanes(x, index):
    return jnp.take_along_axis(x, index, axis=1)


def swap_halves(x):
    return pltpu.roll(x, LANES // 2, axis=1)


def mm(a, b, dims=((1,), (0,)), precision=None):
    return lax.dot_general(a, b, (dims, ((), ())), precision=precision, preferred_element_type=jnp.float32)


def split2(x):
    high = x.astype(jnp.bfloat16)
    return high, (x - high.astype(jnp.float32)).astype(jnp.bfloat16)


def mm_split(a, b):
    (a_high, a_low), (b_high, b_low) = a, b
    return mm(jnp.concatenate([a_high, a_high, a_low], axis=1), jnp.concatenate([b_high, b_low, b_high], axis=0))


def split3(x):
    high = x.astype(jnp.bfloat16).astype(jnp.float32)
    rest = x - high
    mid = rest.astype(jnp.bfloat16).astype(jnp.float32)
    return high, mid, rest - mid


def pack_kernel(rows_ref, points_ref, vectors_ref, leaf_ref, node_ref, out_ref, stage):
    width = vectors_ref.shape[0]
    half = LANES // 2
    low = iota((1, LANES), 1) < half
    stage[...] = jnp.zeros_like(stage)
    stage[0:1, 0:half] = leaf_ref[...].astype(jnp.float32)
    stage[1:5, 0:half] = node_ref[0].astype(jnp.float32)
    stage[5:8, 0:width] = points_ref[...].astype(jnp.float32)
    s = stage[...]
    index = s[0:1]
    index = (index + swap_halves(jnp.broadcast_to(index, (SUB, LANES)))[0:1]).astype(jnp.int32)
    index = jnp.broadcast_to(index, (SUB, LANES))
    stage[0:3, :] = rows_ref[:, 0:LANES]
    found = jnp.zeros((SUB, LANES), jnp.float32)
    for tile in range(rows_ref.shape[1] // LANES):
        stage[0:3, :] = rows_ref[:, tile * LANES : (tile + 1) * LANES]
        picked = take_lanes(stage[...], index & (LANES - 1))
        found = jnp.where(index // LANES == tile, picked, found)
    high, mid, tail = split3(found)
    swapped = swap_halves(s)
    lines = [
        jnp.where(low, high[0:1], mid[0:1]),
        jnp.where(low, tail[0:1], high[1:2]),
        jnp.where(low, mid[1:2], tail[1:2]),
        jnp.where(low, high[2:3], mid[2:3]),
        tail[2:3],
        jnp.where(low, s[1:2], swapped[2:3]),
        jnp.where(low, s[3:4], swapped[4:5]),
        s[5:6] + pltpu.roll(s, width, axis=1)[6:7] + pltpu.roll(s, 2 * width, axis=1)[7:8],
    ]
    block = jnp.concatenate([vectors_ref[...].astype(jnp.float32)] + lines, axis=0).astype(jnp.bfloat16)

    def put(device, unused):
        out_ref[device] = block
        return unused

    lax.fori_loop(0, out_ref.shape[0], put, 0)


def evaluate(dist):
    inverse = lax.rsqrt(dist)
    turns = dist * inverse
    f = turns - jnp.round(turns)
    u = f * f
    scale = math.sqrt(TURNS)
    sine = SIN_POLY[-1] * scale
    cosine = COS_POLY[-1] * scale
    for value in SIN_POLY[-2::-1]:
        sine = sine * u + value * scale
    for value in COS_POLY[-2::-1]:
        cosine = cosine * u + value * scale
    sine = sine * f
    real = (TURNS - sine * sine) * inverse
    imag = (sine * cosine) * inverse
    return real.astype(jnp.bfloat16), imag.astype(jnp.bfloat16)


def main_kernel(levels, got_ref, rows_ref, interp_ref, maps_ref, top_ref, left_ref, kre_ref, kim_ref, samples_ref):
    half = LANES // 2
    leaf = lax.axis_index("rows")
    column = lax.axis_index("cols")
    cols = lax.axis_size("cols")
    group_leaves = 2**levels
    group_devices = group_leaves * cols
    devices = got_ref.shape[0]
    width = got_ref.shape[1] - SUB
    width_bits = width.bit_length() - 1
    lane8 = iota((SUB, LANES), 1)
    sub8 = iota((SUB, LANES), 0)
    low8 = lane8 < half
    member = leaf & (group_leaves - 1)
    mine = sub8 == member >> 1

    group_start = (leaf // group_leaves) * group_devices
    extra = got_ref[pl.ds(group_start, group_devices), width : width + SUB, :].astype(jnp.float32)
    extra = extra.reshape(group_devices * SUB, LANES).astype(jnp.bfloat16)
    shape = (7 * 16, group_devices * SUB)
    at = iota(shape, 0)
    source = ((at & 7) * 2 + ((at >> 3) & 1)) * (cols * SUB) + (at >> 4)
    picked = mm((iota(shape, 1) == source).astype(jnp.bfloat16), extra)
    even = [picked[r * 16 : r * 16 + 8] for r in range(7)]
    odd = [picked[r * 16 + 8 : r * 16 + 16] for r in range(7)]
    even_s = [swap_halves(v) for v in even]
    odd_s = [swap_halves(v) for v in odd]
    coords = [
        jnp.where(low8, even[0] + even_s[0] + even[1], odd[0] + odd_s[0] + odd_s[1]),
        jnp.where(low8, even_s[1] + (even[2] + even_s[2]), odd[1] + (odd[2] + odd_s[2])),
        jnp.where(low8, even[3] + even_s[3] + even[4], odd[3] + odd_s[3] + odd[4]),
    ]
    lists = [
        jnp.where(low8, even[5], even_s[5]).astype(jnp.int32),
        jnp.where(low8, even_s[5], even[5]).astype(jnp.int32),
        jnp.where(low8, even[6], even_s[6]).astype(jnp.int32),
        jnp.where(low8, even_s[6], even[6]).astype(jnp.int32),
    ]

    def own_row(x):
        return jnp.sum(jnp.where(mine, x, jnp.zeros_like(x)), axis=0, keepdims=True)

    siblings = []
    own_lists = [own_row(lists[0])]
    stacked = coords
    for level in range(1, levels):
        own = [take_lanes(v, lists[level - 1]) for v in stacked]
        step = 2 ** (level - 1)
        upper = (sub8 & step) != 0
        other = [jnp.where(upper, pltpu.roll(v, step, axis=0), pltpu.roll(v, SUB - step, axis=0)) for v in own]
        siblings.append([own_row(v) for v in other])
        stacked = [jnp.where(low8 == upper, b, a) for a, b in zip(own, other)]
        own_lists.append(own_row(lists[level]))
    low1 = iota((1, LANES), 1) < half
    tiles = [[own_row(v) for v in coords]]
    tiles.append([jnp.where(low1, a, b) for a, b in zip(siblings[0], siblings[1])])
    tiles.append(siblings[2])
    tree_lanes = len(tiles) * LANES
    own_rows = rows_ref.shape[1] // cols
    start = pl.multiple_of(column * own_rows, LANES)
    own_points = rows_ref[:, pl.ds(start, own_rows)]

    def right_side(points):
        lanes = points[0].shape[1]
        lines = []
        norm = jnp.full((1, lanes), SMOOTH * SMOOTH, jnp.float32)
        for x in points:
            norm = norm + x * x
            lines += split3(x * (-2 * TURNS * TURNS))
        for repeat in range(6):
            lines += [jnp.full((1, lanes), v, jnp.float32) for v in SCALE_PARTS]
        lines += split3(norm * (TURNS * TURNS))
        lines.append(jnp.zeros((LANES - len(lines), lanes), jnp.float32))
        return jnp.concatenate(lines, axis=0).astype(jnp.bfloat16)

    right_tree = jnp.concatenate([right_side(t) for t in tiles], axis=1)
    right_own = right_side([own_points[c : c + 1] for c in range(3)])

    block_devices = min(devices, group_devices)
    single = block_devices == devices
    block = block_devices * width
    vec_count = got_ref.shape[2]
    eye = (iota((vec_count, vec_count), 0) == iota((vec_count, vec_count), 1)).astype(jnp.bfloat16)
    shape = (block, block_devices * SUB)
    spread = (iota(shape, 1) == ((iota(shape, 0) >> width_bits) * SUB + SUB - 1)).astype(jnp.bfloat16)
    shape = (block, LANES)
    lane_of = iota(shape, 1)
    keep = (((lane_of ^ iota(shape, 0)) & (width - 1)) == 0) & (lane_of < 3 * width)
    ones = ((lane_of >= 27) & (lane_of < 30)).astype(jnp.bfloat16)
    shape = (LANES, LANES)
    away = iota(shape, 1) - 3 * (iota(shape, 0) >> width_bits)
    within = iota(shape, 0) < 3 * width
    collect = jnp.concatenate(
        [(within & (away >= first) & (away < first + 3)).astype(jnp.bfloat16) for first in (0, 9, 18)], axis=0
    )

    def panel_vectors(number):
        got = got_ref[pl.ds(number * block_devices, block_devices), 0:width, :].astype(jnp.float32)
        vectors = got.reshape(block, vec_count).astype(jnp.bfloat16)
        return mm(eye, vectors, dims=((1,), (1,))).astype(jnp.bfloat16)

    def panel_left(number):
        tail = got_ref[pl.ds(number * block_devices, block_devices), width : width + SUB, :].astype(jnp.float32)
        tail = tail.reshape(block_devices * SUB, LANES).astype(jnp.bfloat16)
        points = jnp.where(keep, mm(spread, tail), 0.0)
        high, low = split2(points * points)
        left_ref[...] = mm(jnp.concatenate([points.astype(jnp.bfloat16), high, low], axis=1), collect).astype(jnp.bfloat16) + ones

    def fill(at, count, right, lane):
        dist = mm(left_ref[pl.ds(at, count), :], right)
        lanes = right.shape[1]
        kre_ref[pl.ds(at, count), lane : lane + lanes], kim_ref[pl.ds(at, count), lane : lane + lanes] = evaluate(dist)

    def sample(vectors, lane, lanes):
        both = [mm(vectors, k[:, lane : lane + lanes]) for k in (kre_ref, kim_ref)]
        return jnp.concatenate(both, axis=0)

    chunk = min(LANES, block)
    panel_left(0)
    vectors = panel_vectors(0)
    for at in range(0, block, chunk):
        fill(at, chunk, right_tree, 0)
    samples_ref[:, 0:tree_lanes] = sample(vectors, 0, tree_lanes)
    if not single:
        for at in range(0, block, chunk):
            fill(at, chunk, right_own, tree_lanes)
        samples_ref[:, tree_lanes:] = sample(vectors, tree_lanes, own_rows)

        def more(number, unused):
            panel_left(number)
            for at in range(0, block, chunk):
                fill(at, chunk, right_tree, 0)
                fill(at, chunk, right_own, tree_lanes)
            samples_ref[...] += sample(panel_vectors(number), 0, tree_lanes + own_rows)
            return unused

        lax.fori_loop(1, devices // block_devices, more, 0)

    full = (2 * vec_count, LANES)
    low = iota(full, 1) < half
    pair0 = samples_ref[:, 0:LANES]
    pair0_s = swap_halves(pair0)
    pair12 = samples_ref[:, LANES : 2 * LANES]
    pair12_s = swap_halves(pair12)
    pair3 = samples_ref[:, 2 * LANES : 3 * LANES]

    def is_upper(level, shape):
        return (jnp.full(shape, member, jnp.int32) & 2**level) != 0

    upper0 = is_upper(0, full)
    stacks = [pair0]
    skels = [jnp.where(upper0 == low, pair0_s, pair0)]
    for level in range(levels):
        picked = take_lanes(stacks[level], jnp.broadcast_to(own_lists[level], full))
        skels.append(picked)
        if level + 1 < levels:
            up = is_upper(level + 1, full)
            if level == 0:
                other = jnp.where(up, pair12, pair12_s)
            elif level == 1:
                other = jnp.where(up, pair12_s, pair12)
            else:
                other = pair3
            stacks.append(jnp.where(low == up, other, picked))

    two = [jnp.where(low, skels[0], skels[1]).T, jnp.where(low, skels[2], skels[3]).T, skels[4].T]
    row_form = [two[0][0:half], two[0][half:], two[1][0:half], two[1][half:], two[2][0:half]]
    top_ref[0] = row_form[4]
    row_form = [split2(v) for v in row_form]

    stacks = [split2(v) for v in stacks]
    square = (half, LANES)
    low64 = iota(square, 1) < half
    right_maps = [mm_split(row_form[level + 1], stacks[level]) for level in range(levels)]
    gram = mm_split(row_form[0], stacks[0])
    grams = [jnp.where(is_upper(0, square) == low64, swap_halves(gram), gram)]
    for level in range(levels):
        grams.append(take_lanes(right_maps[level], jnp.broadcast_to(own_lists[level], square)))
    pairs = []
    diagonal = iota(square, 0) == (iota(square, 1) & (half - 1))
    for a, b in ((0, 1), (2, 3), (4, 4)):
        gram = jnp.where(low64, grams[a], grams[b])
        trace = jnp.sum(jnp.where(diagonal, gram, 0.0), axis=0, keepdims=True)
        first = jnp.sum(jnp.where(low1, trace, 0.0), axis=1, keepdims=True)
        second = jnp.sum(jnp.where(low1, 0.0, trace), axis=1, keepdims=True)
        trace = jnp.where(low1, first, second)
        ridge = RIDGE * (2 * vec_count) * (trace * (1.0 / (half * 2 * vec_count)) + EPSILON)
        gram = gram + jnp.where(diagonal, ridge, 0.0)
        pairs.append([gram[r * SUB : (r + 1) * SUB] for r in range(half // SUB)])

    where_in_half = lane8 & (half - 1)
    half_base = lane8 - where_in_half
    blocks = half // SUB
    piece = block // blocks

    def spread_row(x, row):
        return jnp.broadcast_to(x[row : row + 1], (SUB, LANES))

    zero8 = jnp.zeros((SUB, LANES), jnp.float32)
    for turn in range(blocks):
        first = turn * SUB
        ahead = turn + 1 if turn + 1 < blocks else None
        within_turn = (where_in_half >> 3) == turn
        diagonals = [[take_lanes(a[turn], half_base + (first + j)) for j in range(SUB)] for a in pairs]
        if ahead is not None:
            nexts = [[take_lanes(a[ahead], half_base + (first + j)) for j in range(SUB)] for a in pairs]
        lines = [a[turn] for a in pairs]
        for s in range(SUB):
            if single and s % 2 == 0:
                fill(turn * piece + s // 2 * (piece // 4), piece // 4, right_own, tree_lanes)
            here = where_in_half == first + s
            row = sub8 == s
            for n in range(len(pairs)):
                columns = diagonals[n]
                inverse = 1.0 / spread_row(columns[s], s)
                column = jnp.where(row, -1.0, columns[s])
                line = jnp.where(here, 1.0, spread_row(lines[n], s)) * inverse
                lines[n] = jnp.where(here | row, 0.0, lines[n]) - column * line
                for j in range(s + 1, SUB):
                    factor = spread_row(columns[j], s) * inverse
                    columns[j] = jnp.where(row, 0.0, columns[j]) - column * factor
        for n, a in enumerate(pairs):
            line = lines[n]
            cleared = [jnp.where(within_turn, 0.0, v) for v in a]
            others = [b for b in range(blocks) if b not in (turn, ahead)]
            if ahead is not None:
                terms = [nexts[n][j] * spread_row(line, j) for j in range(SUB)]
                while len(terms) > 1:
                    terms = [x + y for x, y in zip(terms[::2], terms[1::2])]
            stacked = [zero8] * (2 * blocks)
            stacked[turn] = jnp.where(low8, line, 0.0)
            stacked[blocks + turn] = jnp.where(low8, 0.0, line)
            left = split2(jnp.concatenate([a[b] for b in others], axis=0))
            product = mm_split(left, split2(jnp.concatenate(stacked, axis=0)))
            for number, b in enumerate(others):
                a[b] = cleared[b] - product[number * SUB : (number + 1) * SUB]
            if ahead is not None:
                a[ahead] = cleared[ahead] - terms[0]
            a[turn] = line

    inverses = []
    for a in pairs:
        both = jnp.concatenate(a, axis=0)
        inverses.append(split2(jnp.concatenate([jnp.where(low64, both, 0.0), jnp.where(low64, 0.0, both)], axis=0)))
    if single:
        own_samples = sample(vectors, tree_lanes, own_rows)
    else:
        own_samples = samples_ref[:, tree_lanes:]
    right_leaf = mm_split(row_form[0], split2(own_samples))

    def rows_from(pair, first, last):
        return pair[0][first:last], pair[1][first:last]

    result = mm_split(inverses[1], split2(jnp.concatenate([right_maps[1], right_maps[2]], axis=0)))
    maps_ref[0, 1] = result[0:half]
    maps_ref[0, 2] = result[half:]
    zero = jnp.zeros((half, LANES), jnp.float32)
    maps_ref[0, 3] = mm_split(rows_from(inverses[2], 0, half), split2(jnp.concatenate([right_maps[3], zero], axis=0)))
    maps_ref[0, 0] = mm_split(rows_from(inverses[0], half, LANES), split2(jnp.concatenate([zero, right_maps[0]], axis=0)))
    zero = jnp.zeros((half, own_rows), jnp.float32)
    interp_ref[...] = mm_split(rows_from(inverses[0], 0, half), split2(jnp.concatenate([right_leaf, zero], axis=0)))


def body(row_points, panel_points, test_vectors, leaf_skeleton, node_skeleton):
    devices = lax.axis_size("rows") * lax.axis_size("cols")
    vec_count, width = test_vectors.shape
    rows_here = row_points.shape[1]
    levels, skel = node_skeleton.shape[1:]
    packed = pl.pallas_call(
        pack_kernel,
        out_shape=pltpu.VMEM((devices, width + SUB, vec_count), jnp.bfloat16),
        in_specs=[VMEM] * 5,
        out_specs=VMEM,
        scratch_shapes=[pltpu.VMEM((SUB, LANES), jnp.float32)],
    )(row_points, panel_points, test_vectors.T, leaf_skeleton, node_skeleton)
    got = lax.all_to_all(packed, ("rows", "cols"), 0, 0, tiled=True)
    own_rows = rows_here // lax.axis_size("cols")
    lanes = 3 * LANES + own_rows
    block = min(devices, 2**levels * lax.axis_size("cols")) * width
    return pl.pallas_call(
        functools.partial(main_kernel, levels),
        out_shape=(
            jax.ShapeDtypeStruct((skel, own_rows), jnp.float32),
            jax.ShapeDtypeStruct((1, levels, skel, 2 * skel), jnp.float32),
            jax.ShapeDtypeStruct((1, skel, 2 * vec_count), jnp.float32),
        ),
        in_specs=[VMEM] * 2,
        out_specs=(VMEM, VMEM, VMEM),
        scratch_shapes=[
            pltpu.VMEM((block, LANES), jnp.bfloat16),
            pltpu.VMEM((block, lanes), jnp.bfloat16),
            pltpu.VMEM((block, lanes), jnp.bfloat16),
            pltpu.VMEM((2 * vec_count, lanes), jnp.float32),
        ],
    )(pltpu.with_memory_space_constraint(got, pltpu.VMEM), row_points)


def solution(mesh):
    placed = (
        P(None, "rows"),
        P(None, ("rows", "cols")),
        P(None, ("rows", "cols")),
        P("rows", None),
        P("rows", None, None),
    )
    return jax.shard_map(
        body,
        mesh=mesh,
        in_specs=placed,
        out_specs=(P(None, ("rows", "cols")), P("rows", None, None, None), P("rows", None, None)),
        check_vma=False,
    )
```

```python
import functools
import math

import jax
import jax.numpy as jnp
import numpy as np
from jax import lax
from jax.experimental import pallas as pl
from jax.experimental.pallas import tpu as pltpu
from jax.sharding import PartitionSpec as P

KAPPA = 40.0
SMOOTH = 0.05
RIDGE = 0.1
EPSILON = 1e-05

LANES = 128
SUB = 8
VMEM = pl.BlockSpec(memory_space=pltpu.VMEM)

TURNS = KAPPA / (2 * math.pi)
SIN_POLY = (4.442867902871973, -7.30744341774541, 3.594788055359915, -0.7843739844598376)
COS_POLY = (1.4142134965650128, -6.978850988238946, 5.739461170681512, -1.8835629873012505, 0.31069819181076774)


def bf16_parts(value):
    parts = []
    for unused in range(3):
        parts.append(float(np.float32(value).astype(jnp.bfloat16)))
        value -= parts[-1]
    return parts


SCALE_PARTS = bf16_parts(TURNS * TURNS)


def iota(shape, dim):
    return lax.broadcasted_iota(jnp.int32, shape, dim)


def take_lanes(x, index):
    return jnp.take_along_axis(x, index, axis=1)


def swap_halves(x):
    return pltpu.roll(x, LANES // 2, axis=1)


def mm(a, b, dims=((1,), (0,)), precision=None):
    return lax.dot_general(a, b, (dims, ((), ())), precision=precision, preferred_element_type=jnp.float32)


def split2(x):
    high = x.astype(jnp.bfloat16)
    return high, (x - high.astype(jnp.float32)).astype(jnp.bfloat16)


def mm_split(a, b):
    (a_high, a_low), (b_high, b_low) = a, b
    return mm(jnp.concatenate([a_high, a_high, a_low], axis=1), jnp.concatenate([b_high, b_low, b_high], axis=0))


def split3(x):
    high = x.astype(jnp.bfloat16).astype(jnp.float32)
    rest = x - high
    mid = rest.astype(jnp.bfloat16).astype(jnp.float32)
    return high, mid, rest - mid


def pack_kernel(rows_ref, points_ref, vectors_ref, leaf_ref, node_ref, out_ref, kept_ref, stage):
    kept_ref[...] = rows_ref[...]
    width = vectors_ref.shape[0]
    half = LANES // 2
    low = iota((1, LANES), 1) < half
    stage[...] = jnp.zeros_like(stage)
    stage[0:1, 0:half] = leaf_ref[...].astype(jnp.float32)
    stage[1:5, 0:half] = node_ref[0].astype(jnp.float32)
    stage[5:8, 0:width] = points_ref[...].astype(jnp.float32)
    s = stage[...]
    index = s[0:1]
    index = (index + swap_halves(jnp.broadcast_to(index, (SUB, LANES)))[0:1]).astype(jnp.int32)
    index = jnp.broadcast_to(index, (SUB, LANES))
    stage[0:3, :] = rows_ref[:, 0:LANES]
    found = jnp.zeros((SUB, LANES), jnp.float32)
    for tile in range(rows_ref.shape[1] // LANES):
        stage[0:3, :] = rows_ref[:, tile * LANES : (tile + 1) * LANES]
        picked = take_lanes(stage[...], index & (LANES - 1))
        found = jnp.where(index // LANES == tile, picked, found)
    high, mid, tail = split3(found)
    swapped = swap_halves(s)
    lines = [
        jnp.where(low, high[0:1], mid[0:1]),
        jnp.where(low, tail[0:1], high[1:2]),
        jnp.where(low, mid[1:2], tail[1:2]),
        jnp.where(low, high[2:3], mid[2:3]),
        tail[2:3],
        jnp.where(low, s[1:2], swapped[2:3]),
        jnp.where(low, s[3:4], swapped[4:5]),
        s[5:6] + pltpu.roll(s, width, axis=1)[6:7] + pltpu.roll(s, 2 * width, axis=1)[7:8],
    ]
    block = jnp.concatenate([vectors_ref[...].astype(jnp.float32)] + lines, axis=0).astype(jnp.bfloat16)

    def put(device, unused):
        out_ref[device] = block
        return unused

    lax.fori_loop(0, out_ref.shape[0], put, 0)


SETUP_PIECES = 4
STAGE_PIECES = 4
TURN_PIECES = (0, 0, 0, 0, 0, 0, 0, 0)
LEAF_TURN = 3


def evaluate(dist):
    inverse = lax.rsqrt(dist)
    turns = dist * inverse
    f = turns - jnp.round(turns)
    u = f * f
    scale = math.sqrt(TURNS)
    sine = SIN_POLY[-1] * scale
    cosine = COS_POLY[-1] * scale
    for value in SIN_POLY[-2::-1]:
        sine = sine * u + value * scale
    for value in COS_POLY[-2::-1]:
        cosine = cosine * u + value * scale
    sine = sine * f
    real = (TURNS - sine * sine) * inverse
    imag = (sine * cosine) * inverse
    return real.astype(jnp.bfloat16), imag.astype(jnp.bfloat16)


def main_kernel(levels, got_ref, rows_ref, interp_ref, maps_ref, top_ref, left_ref, kre_ref, kim_ref, samples_ref):
    half = LANES // 2
    leaf = lax.axis_index("rows")
    column = lax.axis_index("cols")
    cols = lax.axis_size("cols")
    group_leaves = 2**levels
    group_devices = group_leaves * cols
    devices = got_ref.shape[0]
    width = got_ref.shape[1] - SUB
    width_bits = width.bit_length() - 1
    lane8 = iota((SUB, LANES), 1)
    sub8 = iota((SUB, LANES), 0)
    low8 = lane8 < half
    member = leaf & (group_leaves - 1)
    mine = sub8 == member >> 1

    tree_lanes = 3 * LANES
    own_rows = rows_ref.shape[1] // cols
    start = pl.multiple_of(column * own_rows, LANES)
    own_points = rows_ref[:, pl.ds(start, own_rows)]

    def right_side(points):
        lanes = points[0].shape[1]
        lines = []
        norm = jnp.full((1, lanes), SMOOTH * SMOOTH, jnp.float32)
        for x in points:
            norm = norm + x * x
            lines += split3(x * (-2 * TURNS * TURNS))
        for repeat in range(6):
            lines += [jnp.full((1, lanes), v, jnp.float32) for v in SCALE_PARTS]
        lines += split3(norm * (TURNS * TURNS))
        lines.append(jnp.zeros((LANES - len(lines), lanes), jnp.float32))
        return jnp.concatenate(lines, axis=0).astype(jnp.bfloat16)

    block_devices = min(devices, group_devices)
    single = block_devices == devices
    block = block_devices * width
    vec_count = got_ref.shape[2]
    eye = (iota((vec_count, vec_count), 0) == iota((vec_count, vec_count), 1)).astype(jnp.bfloat16)
    shape = (width, LANES)
    lane_of = iota(shape, 1)
    keep = (((lane_of ^ iota(shape, 0)) & (width - 1)) == 0) & (lane_of < 3 * width)
    ones = ((iota((1, LANES), 1) >= 27) & (iota((1, LANES), 1) < 30)).astype(jnp.float32)
    shape = (LANES, LANES)
    away = iota(shape, 1) - 3 * (iota(shape, 0) >> width_bits)
    within = iota(shape, 0) < 3 * width
    collect = jnp.concatenate(
        [(within & (away >= first) & (away < first + 3)).astype(jnp.bfloat16) for first in (0, 9, 18)], axis=0
    )

    def panel_vectors(number):
        got = got_ref[pl.ds(number * block_devices, block_devices), 0:width, :].astype(jnp.float32)
        vectors = got.reshape(block, vec_count).astype(jnp.bfloat16)
        return mm(eye, vectors, dims=((1,), (1,))).astype(jnp.bfloat16)

    def panel_left(number):
        tail = got_ref[pl.ds(number * block_devices, block_devices), width : width + SUB, :].astype(jnp.float32)
        points = [jnp.where(keep, jnp.broadcast_to(tail[d, SUB - 1 : SUB], keep.shape), 0.0) for d in range(block_devices)]
        points = jnp.concatenate(points, axis=0)
        high, low = split2(points * points)
        left = mm(jnp.concatenate([points.astype(jnp.bfloat16), high, low], axis=1), collect) + ones
        left_ref[...] = left.astype(jnp.bfloat16)

    def fill(at, count, right, lane):
        dist = mm(left_ref[pl.ds(at, count), :], right)
        lanes = right.shape[1]
        kre_ref[pl.ds(at, count), lane : lane + lanes], kim_ref[pl.ds(at, count), lane : lane + lanes] = evaluate(dist)

    def sample(vectors, lane, lanes):
        both = [mm(vectors, k[:, lane : lane + lanes]) for k in (kre_ref, kim_ref)]
        return jnp.concatenate(both, axis=0)

    chunk = min(LANES, block)
    panel_left(0)
    right_own = right_side([own_points[c : c + 1] for c in range(3)])
    pieces = list(range(0, block, 16)) if single else []

    def own_pieces(count):
        for unused in range(min(count, len(pieces))):
            fill(pieces.pop(0), 16, right_own, tree_lanes)

    vectors = panel_vectors(0)
    group_start = (leaf // group_leaves) * group_devices
    extra = got_ref[pl.ds(group_start, group_devices), width : width + SUB, :].astype(jnp.float32)
    extra = extra.reshape(group_devices * SUB, LANES).astype(jnp.bfloat16)
    shape = (7 * 16, group_devices * SUB)
    at = iota(shape, 0)
    source = ((at & 7) * 2 + ((at >> 3) & 1)) * (cols * SUB) + (at >> 4)
    picked = mm((iota(shape, 1) == source).astype(jnp.bfloat16), extra)
    even = [picked[r * 16 : r * 16 + 8] for r in range(7)]
    odd = [picked[r * 16 + 8 : r * 16 + 16] for r in range(7)]
    even_s = [swap_halves(v) for v in even]
    odd_s = [swap_halves(v) for v in odd]
    coords = [
        jnp.where(low8, even[0] + even_s[0] + even[1], odd[0] + odd_s[0] + odd_s[1]),
        jnp.where(low8, even_s[1] + (even[2] + even_s[2]), odd[1] + (odd[2] + odd_s[2])),
        jnp.where(low8, even[3] + even_s[3] + even[4], odd[3] + odd_s[3] + odd[4]),
    ]
    lists = [
        jnp.where(low8, even[5], even_s[5]).astype(jnp.int32),
        jnp.where(low8, even_s[5], even[5]).astype(jnp.int32),
        jnp.where(low8, even[6], even_s[6]).astype(jnp.int32),
        jnp.where(low8, even_s[6], even[6]).astype(jnp.int32),
    ]

    def own_row(x):
        return jnp.sum(jnp.where(mine, x, jnp.zeros_like(x)), axis=0, keepdims=True)

    siblings = []
    own_lists = [own_row(lists[0])]
    stacked = coords
    for level in range(1, levels):
        own = [take_lanes(v, lists[level - 1]) for v in stacked]
        step = 2 ** (level - 1)
        upper = (sub8 & step) != 0
        other = [jnp.where(upper, pltpu.roll(v, step, axis=0), pltpu.roll(v, SUB - step, axis=0)) for v in own]
        siblings.append([own_row(v) for v in other])
        stacked = [jnp.where(low8 == upper, b, a) for a, b in zip(own, other)]
        own_lists.append(own_row(lists[level]))
        own_pieces(SETUP_PIECES)
    low1 = iota((1, LANES), 1) < half
    tiles = [[own_row(v) for v in coords]]
    tiles.append([jnp.where(low1, a, b) for a, b in zip(siblings[0], siblings[1])])
    tiles.append(siblings[2])
    right_tree = jnp.concatenate([right_side(t) for t in tiles], axis=1)

    for at in range(0, block, chunk):
        fill(at, chunk, right_tree, 0)
    samples_ref[:, 0:tree_lanes] = sample(vectors, 0, tree_lanes)
    if not single:
        for at in range(0, block, chunk):
            fill(at, chunk, right_own, tree_lanes)
        samples_ref[:, tree_lanes:] = sample(vectors, tree_lanes, own_rows)

        def more(number, unused):
            panel_left(number)
            for at in range(0, block, chunk):
                fill(at, chunk, right_tree, 0)
                fill(at, chunk, right_own, tree_lanes)
            samples_ref[...] += sample(panel_vectors(number), 0, tree_lanes + own_rows)
            return unused

        lax.fori_loop(1, devices // block_devices, more, 0)

    full = (2 * vec_count, LANES)
    low = iota(full, 1) < half
    pair0 = samples_ref[:, 0:LANES]
    pair0_s = swap_halves(pair0)
    pair12 = samples_ref[:, LANES : 2 * LANES]
    pair12_s = swap_halves(pair12)
    pair3 = samples_ref[:, 2 * LANES : 3 * LANES]

    def is_upper(level, shape):
        return (jnp.full(shape, member, jnp.int32) & 2**level) != 0

    upper0 = is_upper(0, full)
    stacks = [pair0]
    skels = [jnp.where(upper0 == low, pair0_s, pair0)]
    for level in range(levels):
        picked = take_lanes(stacks[level], jnp.broadcast_to(own_lists[level], full))
        skels.append(picked)
        own_pieces(STAGE_PIECES)
        if level + 1 < levels:
            up = is_upper(level + 1, full)
            if level == 0:
                other = jnp.where(up, pair12, pair12_s)
            elif level == 1:
                other = jnp.where(up, pair12_s, pair12)
            else:
                other = pair3
            stacks.append(jnp.where(low == up, other, picked))

    two = [jnp.where(low, skels[0], skels[1]).T, jnp.where(low, skels[2], skels[3]).T, skels[4].T]
    row_form = [two[0][0:half], two[0][half:], two[1][0:half], two[1][half:], two[2][0:half]]
    top_ref[0] = row_form[4]
    row_form = [split2(v) for v in row_form]

    stacks = [split2(v) for v in stacks]
    square = (half, LANES)
    low64 = iota(square, 1) < half
    right_maps = [mm_split(row_form[level + 1], stacks[level]) for level in range(levels)]
    gram = mm_split(row_form[0], stacks[0])
    grams = [jnp.where(is_upper(0, square) == low64, swap_halves(gram), gram)]
    for level in range(levels):
        grams.append(take_lanes(right_maps[level], jnp.broadcast_to(own_lists[level], square)))
    pairs = []
    diagonal = iota(square, 0) == (iota(square, 1) & (half - 1))
    for a, b in ((0, 1), (2, 3), (4, 4)):
        gram = jnp.where(low64, grams[a], grams[b])
        trace = jnp.sum(jnp.where(diagonal, gram, 0.0), axis=0, keepdims=True)
        first = jnp.sum(jnp.where(low1, trace, 0.0), axis=1, keepdims=True)
        second = jnp.sum(jnp.where(low1, 0.0, trace), axis=1, keepdims=True)
        trace = jnp.where(low1, first, second)
        ridge = RIDGE * (2 * vec_count) * (trace * (1.0 / (half * 2 * vec_count)) + EPSILON)
        gram = gram + jnp.where(diagonal, ridge, 0.0)
        pairs.append([gram[r * SUB : (r + 1) * SUB] for r in range(half // SUB)])

    right_maps = [split2(v) for v in right_maps]
    where_in_half = lane8 & (half - 1)
    half_base = lane8 - where_in_half
    blocks = half // SUB

    def spread_row(x, row):
        return jnp.broadcast_to(x[row : row + 1], (SUB, LANES))

    def total_of(terms):
        while len(terms) > 1:
            terms = [x + y for x, y in zip(terms[::2], terms[1::2])]
        return terms[0]

    zero8 = jnp.zeros((SUB, LANES), jnp.float32)
    zero16 = jnp.zeros((2 * SUB, LANES), jnp.bfloat16)
    for turn in range(blocks):
        first = turn * SUB
        ahead = turn + 1 if turn + 1 < blocks else None
        within_turn = (where_in_half >> 3) == turn
        diagonals = [[take_lanes(a[turn], half_base + (first + j)) for j in range(SUB)] for a in pairs]
        if ahead is not None:
            nexts = [[take_lanes(a[ahead], half_base + (first + j)) for j in range(SUB)] for a in pairs]
        lines = [a[turn] for a in pairs]
        for s in range(SUB):
            own_pieces(TURN_PIECES[turn] if s % 2 == 0 else 0)
            here = where_in_half == first + s
            row = sub8 == s
            pivots = [spread_row(columns[s], s) for columns in diagonals]
            inverses = 1.0 / jnp.where(sub8 == 0, pivots[0], jnp.where(sub8 == 1, pivots[1], pivots[2]))
            for n in range(len(pairs)):
                columns = diagonals[n]
                inverse = spread_row(inverses, n)
                column = jnp.where(row, -1.0, columns[s])
                line = jnp.where(here, 1.0, spread_row(lines[n], s)) * inverse
                lines[n] = jnp.where(here | row, 0.0, lines[n]) - column * line
                for j in range(s + 1, SUB):
                    factor = spread_row(columns[j], s) * inverse
                    columns[j] = jnp.where(row, 0.0, columns[j]) - column * factor
        if turn == LEAF_TURN:
            own_pieces(block)
            own_samples = sample(vectors, tree_lanes, own_rows) if single else samples_ref[:, tree_lanes:]
            right_leaf = split2(mm_split(row_form[0], split2(own_samples)))
        for n, a in enumerate(pairs):
            line = lines[n]
            cleared = [jnp.where(within_turn, 0.0, v) for v in a]
            others = [b for b in range(blocks) if b not in (turn, ahead)]
            if ahead is not None:
                a[ahead] = cleared[ahead] - total_of([nexts[n][j] * spread_row(line, j) for j in range(SUB)])

            def placed(part):
                pads = [zero16] * blocks
                both = [part, zero8] if turn % 2 == 0 else [zero8, part]
                for side, chosen in ((0, low8), (1, ~low8)):
                    pads[side * blocks // 2 + turn // 2] = jnp.concatenate(
                        [jnp.where(chosen, v, 0.0) for v in both], axis=0
                    ).astype(jnp.bfloat16)
                return jnp.concatenate(pads, axis=0)

            high = line.astype(jnp.bfloat16).astype(jnp.float32)
            right = placed(high), placed(line - high)
            product = mm_split(split2(jnp.concatenate([a[b] for b in others], axis=0)), right)
            for number, b in enumerate(others):
                a[b] = cleared[b] - product[number * SUB : (number + 1) * SUB]
            a[turn] = line

    inverses = []
    for a in pairs:
        both = jnp.concatenate(a, axis=0)
        inverses.append(split2(jnp.concatenate([jnp.where(low64, both, 0.0), jnp.where(low64, 0.0, both)], axis=0)))
    def times(pair, first, last, parts):
        left = [v[first:last] for v in pair]
        return mm_split(left, [jnp.concatenate(p, axis=0) if len(p) > 1 else p[0] for p in zip(*parts)])

    zero = [jnp.zeros((half, LANES), jnp.bfloat16)] * 2
    wide = [jnp.zeros((half, own_rows), jnp.bfloat16)] * 2
    result = times(inverses[1], 0, LANES, (right_maps[1], right_maps[2]))
    maps_ref[0, 1] = result[0:half]
    maps_ref[0, 2] = result[half:]
    maps_ref[0, 3] = times(inverses[2], 0, half, (right_maps[3], zero))
    maps_ref[0, 0] = times(inverses[0], half, LANES, (zero, right_maps[0]))
    interp_ref[...] = times(inverses[0], 0, half, (right_leaf, wide))


def body(row_points, panel_points, test_vectors, leaf_skeleton, node_skeleton):
    devices = lax.axis_size("rows") * lax.axis_size("cols")
    vec_count, width = test_vectors.shape
    rows_here = row_points.shape[1]
    levels, skel = node_skeleton.shape[1:]
    packed, kept = pl.pallas_call(
        pack_kernel,
        out_shape=(
            pltpu.VMEM((devices, width + SUB, vec_count), jnp.bfloat16),
            pltpu.VMEM(row_points.shape, jnp.float32),
        ),
        in_specs=[VMEM] * 5,
        out_specs=(VMEM, VMEM),
        scratch_shapes=[pltpu.VMEM((SUB, LANES), jnp.float32)],
    )(row_points, panel_points, test_vectors.T, leaf_skeleton, node_skeleton)
    got = lax.all_to_all(packed, ("rows", "cols"), 0, 0, tiled=True)
    own_rows = rows_here // lax.axis_size("cols")
    lanes = 3 * LANES + own_rows
    block = min(devices, 2**levels * lax.axis_size("cols")) * width
    return pl.pallas_call(
        functools.partial(main_kernel, levels),
        out_shape=(
            jax.ShapeDtypeStruct((skel, own_rows), jnp.float32),
            jax.ShapeDtypeStruct((1, levels, skel, 2 * skel), jnp.float32),
            jax.ShapeDtypeStruct((1, skel, 2 * vec_count), jnp.float32),
        ),
        in_specs=[VMEM] * 2,
        out_specs=(VMEM, VMEM, VMEM),
        scratch_shapes=[
            pltpu.VMEM((block, LANES), jnp.bfloat16),
            pltpu.VMEM((block, lanes), jnp.bfloat16),
            pltpu.VMEM((block, lanes), jnp.bfloat16),
            pltpu.VMEM((2 * vec_count, lanes), jnp.float32),
        ],
    )(pltpu.with_memory_space_constraint(got, pltpu.VMEM), pltpu.with_memory_space_constraint(kept, pltpu.VMEM))


def solution(mesh):
    placed = (
        P(None, "rows"),
        P(None, ("rows", "cols")),
        P(None, ("rows", "cols")),
        P("rows", None),
        P("rows", None, None),
    )
    return jax.shard_map(
        body,
        mesh=mesh,
        in_specs=placed,
        out_specs=(P(None, ("rows", "cols")), P("rows", None, None, None), P("rows", None, None)),
        check_vma=False,
    )
```

```python
import functools
import math

import jax
import jax.numpy as jnp
import numpy as np
from jax import lax
from jax.experimental import pallas as pl
from jax.experimental.pallas import tpu as pltpu
from jax.sharding import PartitionSpec as P

KAPPA = 40.0
SMOOTH = 0.05
RIDGE = 0.1
EPSILON = 1e-05

LANES = 128
SUB = 8
VMEM = pl.BlockSpec(memory_space=pltpu.VMEM)

TURNS = KAPPA / (2 * math.pi)
SIN_POLY = (4.442867902871973, -7.30744341774541, 3.594788055359915, -0.7843739844598376)
COS_POLY = (1.4142134965650128, -6.978850988238946, 5.739461170681512, -1.8835629873012505, 0.31069819181076774)


def bf16_parts(value):
    parts = []
    for unused in range(3):
        parts.append(float(np.float32(value).astype(jnp.bfloat16)))
        value -= parts[-1]
    return parts


SCALE_PARTS = bf16_parts(TURNS * TURNS)


def iota(shape, dim):
    return lax.broadcasted_iota(jnp.int32, shape, dim)


def take_lanes(x, index):
    return jnp.take_along_axis(x, index, axis=1)


def swap_halves(x):
    return pltpu.roll(x, LANES // 2, axis=1)


def mm(a, b, dims=((1,), (0,)), precision=None):
    return lax.dot_general(a, b, (dims, ((), ())), precision=precision, preferred_element_type=jnp.float32)


def split2(x):
    high = x.astype(jnp.bfloat16)
    return high, (x - high.astype(jnp.float32)).astype(jnp.bfloat16)


def mm_split(a, b):
    (a_high, a_low), (b_high, b_low) = a, b
    return mm(jnp.concatenate([a_high, a_high, a_low], axis=1), jnp.concatenate([b_high, b_low, b_high], axis=0))


def split3(x):
    high = x.astype(jnp.bfloat16).astype(jnp.float32)
    rest = x - high
    mid = rest.astype(jnp.bfloat16).astype(jnp.float32)
    return high, mid, rest - mid


def pack_kernel(rows_ref, points_ref, vectors_ref, leaf_ref, node_ref, out_ref, kept_ref, stage):
    kept_ref[...] = rows_ref[...]
    width = vectors_ref.shape[0]
    half = LANES // 2
    low = iota((1, LANES), 1) < half
    stage[...] = jnp.zeros_like(stage)
    stage[0:1, 0:half] = leaf_ref[...].astype(jnp.float32)
    stage[1:5, 0:half] = node_ref[0].astype(jnp.float32)
    stage[5:8, 0:width] = points_ref[...].astype(jnp.float32)
    s = stage[...]
    index = s[0:1]
    index = (index + swap_halves(jnp.broadcast_to(index, (SUB, LANES)))[0:1]).astype(jnp.int32)
    index = jnp.broadcast_to(index, (SUB, LANES))
    stage[0:3, :] = rows_ref[:, 0:LANES]
    found = jnp.zeros((SUB, LANES), jnp.float32)
    for tile in range(rows_ref.shape[1] // LANES):
        stage[0:3, :] = rows_ref[:, tile * LANES : (tile + 1) * LANES]
        picked = take_lanes(stage[...], index & (LANES - 1))
        found = jnp.where(index // LANES == tile, picked, found)
    high, mid, tail = split3(found)
    swapped = swap_halves(s)
    lines = [
        jnp.where(low, high[0:1], mid[0:1]),
        jnp.where(low, tail[0:1], high[1:2]),
        jnp.where(low, mid[1:2], tail[1:2]),
        jnp.where(low, high[2:3], mid[2:3]),
        tail[2:3],
        jnp.where(low, s[1:2], swapped[2:3]),
        jnp.where(low, s[3:4], swapped[4:5]),
        s[5:6] + pltpu.roll(s, width, axis=1)[6:7] + pltpu.roll(s, 2 * width, axis=1)[7:8],
    ]
    block = jnp.concatenate([vectors_ref[...].astype(jnp.float32)] + lines, axis=0).astype(jnp.bfloat16)

    def put(device, unused):
        out_ref[device] = block
        return unused

    lax.fori_loop(0, out_ref.shape[0], put, 0)


SETUP_PIECES = 4
STAGE_PIECES = 4
TURN_PIECES = (0, 0, 0, 0, 0, 0, 0, 0)
LEAF_TURN = 3


def evaluate(dist):
    inverse = lax.rsqrt(dist)
    turns = dist * inverse
    f = turns - jnp.round(turns)
    u = f * f
    scale = math.sqrt(TURNS)
    sine = SIN_POLY[-1] * scale
    cosine = COS_POLY[-1] * scale
    for value in SIN_POLY[-2::-1]:
        sine = sine * u + value * scale
    for value in COS_POLY[-2::-1]:
        cosine = cosine * u + value * scale
    sine = sine * f
    real = (TURNS - sine * sine) * inverse
    imag = (sine * cosine) * inverse
    return real.astype(jnp.bfloat16), imag.astype(jnp.bfloat16)


def main_kernel(levels, got_ref, rows_ref, interp_out, maps_out, top_out, interp_ref, maps_ref, top_ref, left_ref, kre_ref, kim_ref, samples_ref, sems):
    half = LANES // 2
    leaf = lax.axis_index("rows")
    column = lax.axis_index("cols")
    cols = lax.axis_size("cols")
    group_leaves = 2**levels
    group_devices = group_leaves * cols
    devices = got_ref.shape[0]
    width = got_ref.shape[1] - SUB
    width_bits = width.bit_length() - 1
    lane8 = iota((SUB, LANES), 1)
    sub8 = iota((SUB, LANES), 0)
    low8 = lane8 < half
    member = leaf & (group_leaves - 1)
    mine = sub8 == member >> 1

    tree_lanes = 3 * LANES
    own_rows = rows_ref.shape[1] // cols
    start = pl.multiple_of(column * own_rows, LANES)
    own_points = rows_ref[:, pl.ds(start, own_rows)]

    def right_side(points):
        lanes = points[0].shape[1]
        lines = []
        norm = jnp.full((1, lanes), SMOOTH * SMOOTH, jnp.float32)
        for x in points:
            norm = norm + x * x
            lines += split3(x * (-2 * TURNS * TURNS))
        for repeat in range(6):
            lines += [jnp.full((1, lanes), v, jnp.float32) for v in SCALE_PARTS]
        lines += split3(norm * (TURNS * TURNS))
        lines.append(jnp.zeros((LANES - len(lines), lanes), jnp.float32))
        return jnp.concatenate(lines, axis=0).astype(jnp.bfloat16)

    block_devices = min(devices, group_devices)
    single = block_devices == devices
    block = block_devices * width
    vec_count = got_ref.shape[2]
    eye = (iota((vec_count, vec_count), 0) == iota((vec_count, vec_count), 1)).astype(jnp.bfloat16)
    shape = (width, LANES)
    lane_of = iota(shape, 1)
    keep = (((lane_of ^ iota(shape, 0)) & (width - 1)) == 0) & (lane_of < 3 * width)
    ones = ((iota((1, LANES), 1) >= 27) & (iota((1, LANES), 1) < 30)).astype(jnp.float32)
    shape = (LANES, LANES)
    away = iota(shape, 1) - 3 * (iota(shape, 0) >> width_bits)
    within = iota(shape, 0) < 3 * width
    collect = jnp.concatenate(
        [(within & (away >= first) & (away < first + 3)).astype(jnp.bfloat16) for first in (0, 9, 18)], axis=0
    )

    def panel_vectors(number):
        got = got_ref[pl.ds(number * block_devices, block_devices), 0:width, :].astype(jnp.float32)
        vectors = got.reshape(block, vec_count).astype(jnp.bfloat16)
        return mm(eye, vectors, dims=((1,), (1,))).astype(jnp.bfloat16)

    def panel_left(number):
        tail = got_ref[pl.ds(number * block_devices, block_devices), width : width + SUB, :].astype(jnp.float32)
        points = [jnp.where(keep, jnp.broadcast_to(tail[d, SUB - 1 : SUB], keep.shape), 0.0) for d in range(block_devices)]
        points = jnp.concatenate(points, axis=0)
        high, low = split2(points * points)
        left = mm(jnp.concatenate([points.astype(jnp.bfloat16), high, low], axis=1), collect) + ones
        left_ref[...] = left.astype(jnp.bfloat16)

    def fill(at, count, right, lane):
        dist = mm(left_ref[pl.ds(at, count), :], right)
        lanes = right.shape[1]
        kre_ref[pl.ds(at, count), lane : lane + lanes], kim_ref[pl.ds(at, count), lane : lane + lanes] = evaluate(dist)

    def sample(vectors, lane, lanes):
        both = [mm(vectors, k[:, lane : lane + lanes]) for k in (kre_ref, kim_ref)]
        return jnp.concatenate(both, axis=0)

    chunk = min(LANES, block)
    panel_left(0)
    right_own = right_side([own_points[c : c + 1] for c in range(3)])
    pieces = list(range(0, block, 16)) if single else []

    def own_pieces(count):
        for unused in range(min(count, len(pieces))):
            fill(pieces.pop(0), 16, right_own, tree_lanes)

    vectors = panel_vectors(0)
    group_start = (leaf // group_leaves) * group_devices
    extra = got_ref[pl.ds(group_start, group_devices), width : width + SUB, :].astype(jnp.float32)
    extra = extra.reshape(group_devices * SUB, LANES).astype(jnp.bfloat16)
    shape = (7 * 16, group_devices * SUB)
    at = iota(shape, 0)
    source = ((at & 7) * 2 + ((at >> 3) & 1)) * (cols * SUB) + (at >> 4)
    picked = mm((iota(shape, 1) == source).astype(jnp.bfloat16), extra)
    even = [picked[r * 16 : r * 16 + 8] for r in range(7)]
    odd = [picked[r * 16 + 8 : r * 16 + 16] for r in range(7)]
    even_s = [swap_halves(v) for v in even]
    odd_s = [swap_halves(v) for v in odd]
    coords = [
        jnp.where(low8, even[0] + even_s[0] + even[1], odd[0] + odd_s[0] + odd_s[1]),
        jnp.where(low8, even_s[1] + (even[2] + even_s[2]), odd[1] + (odd[2] + odd_s[2])),
        jnp.where(low8, even[3] + even_s[3] + even[4], odd[3] + odd_s[3] + odd[4]),
    ]
    lists = [
        jnp.where(low8, even[5], even_s[5]).astype(jnp.int32),
        jnp.where(low8, even_s[5], even[5]).astype(jnp.int32),
        jnp.where(low8, even[6], even_s[6]).astype(jnp.int32),
        jnp.where(low8, even_s[6], even[6]).astype(jnp.int32),
    ]

    def own_row(x):
        return jnp.sum(jnp.where(mine, x, jnp.zeros_like(x)), axis=0, keepdims=True)

    siblings = []
    own_lists = [own_row(lists[0])]
    stacked = coords
    for level in range(1, levels):
        own = [take_lanes(v, lists[level - 1]) for v in stacked]
        step = 2 ** (level - 1)
        upper = (sub8 & step) != 0
        other = [jnp.where(upper, pltpu.roll(v, step, axis=0), pltpu.roll(v, SUB - step, axis=0)) for v in own]
        siblings.append([own_row(v) for v in other])
        stacked = [jnp.where(low8 == upper, b, a) for a, b in zip(own, other)]
        own_lists.append(own_row(lists[level]))
        own_pieces(SETUP_PIECES)
    low1 = iota((1, LANES), 1) < half
    tiles = [[own_row(v) for v in coords]]
    tiles.append([jnp.where(low1, a, b) for a, b in zip(siblings[0], siblings[1])])
    tiles.append(siblings[2])
    right_tree = jnp.concatenate([right_side(t) for t in tiles], axis=1)

    for at in range(0, block, chunk):
        fill(at, chunk, right_tree, 0)
    samples_ref[:, 0:tree_lanes] = sample(vectors, 0, tree_lanes)
    if not single:
        for at in range(0, block, chunk):
            fill(at, chunk, right_own, tree_lanes)
        samples_ref[:, tree_lanes:] = sample(vectors, tree_lanes, own_rows)

        def more(number, unused):
            panel_left(number)
            for at in range(0, block, chunk):
                fill(at, chunk, right_tree, 0)
                fill(at, chunk, right_own, tree_lanes)
            samples_ref[...] += sample(panel_vectors(number), 0, tree_lanes + own_rows)
            return unused

        lax.fori_loop(1, devices // block_devices, more, 0)

    full = (2 * vec_count, LANES)
    low = iota(full, 1) < half
    pair0 = samples_ref[:, 0:LANES]
    pair0_s = swap_halves(pair0)
    pair12 = samples_ref[:, LANES : 2 * LANES]
    pair12_s = swap_halves(pair12)
    pair3 = samples_ref[:, 2 * LANES : 3 * LANES]

    def is_upper(level, shape):
        return (jnp.full(shape, member, jnp.int32) & 2**level) != 0

    upper0 = is_upper(0, full)
    stacks = [pair0]
    skels = [jnp.where(upper0 == low, pair0_s, pair0)]
    for level in range(levels):
        picked = take_lanes(stacks[level], jnp.broadcast_to(own_lists[level], full))
        skels.append(picked)
        own_pieces(STAGE_PIECES)
        if level + 1 < levels:
            up = is_upper(level + 1, full)
            if level == 0:
                other = jnp.where(up, pair12, pair12_s)
            elif level == 1:
                other = jnp.where(up, pair12_s, pair12)
            else:
                other = pair3
            stacks.append(jnp.where(low == up, other, picked))

    two = [jnp.where(low, skels[0], skels[1]).T, jnp.where(low, skels[2], skels[3]).T, skels[4].T]
    row_form = [two[0][0:half], two[0][half:], two[1][0:half], two[1][half:], two[2][0:half]]
    top_ref[0] = row_form[4]
    copies = []

    def send(source, target):
        copies.append(pltpu.make_async_copy(source, target, sems.at[len(copies)]))
        copies[-1].start()

    send(top_ref, top_out)
    row_form = [split2(v) for v in row_form]

    stacks = [split2(v) for v in stacks]
    square = (half, LANES)
    low64 = iota(square, 1) < half
    right_maps = [mm_split(row_form[level + 1], stacks[level]) for level in range(levels)]
    gram = mm_split(row_form[0], stacks[0])
    grams = [jnp.where(is_upper(0, square) == low64, swap_halves(gram), gram)]
    for level in range(levels):
        grams.append(take_lanes(right_maps[level], jnp.broadcast_to(own_lists[level], square)))
    pairs = []
    scales = []
    diagonal = iota(square, 0) == (iota(square, 1) & (half - 1))
    for a, b in ((0, 1), (2, 3), (4, 4)):
        gram = jnp.where(low64, grams[a], grams[b])
        trace = jnp.sum(jnp.where(diagonal, gram, 0.0), axis=0, keepdims=True)
        first = jnp.sum(jnp.where(low1, trace, 0.0), axis=1, keepdims=True)
        second = jnp.sum(jnp.where(low1, 0.0, trace), axis=1, keepdims=True)
        trace = jnp.where(low1, first, second)
        ridge = RIDGE * (2 * vec_count) * (trace * (1.0 / (half * 2 * vec_count)) + EPSILON)
        scales.append(RIDGE / ridge)
        gram = gram * scales[-1] + jnp.where(diagonal, RIDGE, 0.0)
        pairs.append([gram[r * SUB : (r + 1) * SUB] for r in range(half // SUB)])

    right_maps = [split2(v) for v in right_maps]
    where_in_half = lane8 & (half - 1)
    half_base = lane8 - where_in_half
    blocks = half // SUB

    def spread_row(x, row):
        return jnp.broadcast_to(x[row : row + 1], (SUB, LANES))

    def total_of(terms):
        while len(terms) > 1:
            terms = [x + y for x, y in zip(terms[::2], terms[1::2])]
        return terms[0]

    zero8 = jnp.zeros((SUB, LANES), jnp.float32)
    zero16 = jnp.zeros((2 * SUB, LANES), jnp.bfloat16)
    for turn in range(blocks):
        first = turn * SUB
        ahead = turn + 1 if turn + 1 < blocks else None
        within_turn = (where_in_half >> 3) == turn
        diagonals = [[take_lanes(a[turn], half_base + (first + j)) for j in range(SUB)] for a in pairs]
        if ahead is not None:
            nexts = [[take_lanes(a[ahead], half_base + (first + j)) for j in range(SUB)] for a in pairs]
        lines = [a[turn] for a in pairs]
        for s in range(SUB):
            own_pieces(TURN_PIECES[turn] if s % 2 == 0 else 0)
            here = where_in_half == first + s
            unit = jnp.where(sub8 == s, 1.0, 0.0)
            pivots = [spread_row(columns[s], s) for columns in diagonals]
            inverses = 1.0 / jnp.where(sub8 == 0, pivots[0], jnp.where(sub8 == 1, pivots[1], pivots[2]))
            for n in range(len(pairs)):
                columns = diagonals[n]
                inverse = spread_row(inverses, n)
                column = (columns[s] - unit) * inverse
                line = jnp.where(here, 1.0, spread_row(lines[n], s))
                lines[n] = jnp.where(here, unit, lines[n]) - column * line
                for j in range(s + 1, SUB):
                    columns[j] = columns[j] - column * spread_row(columns[j], s)
        if turn == LEAF_TURN:
            own_pieces(block)
            own_samples = sample(vectors, tree_lanes, own_rows) if single else samples_ref[:, tree_lanes:]
            right_leaf = split2(mm_split(row_form[0], split2(own_samples)))
        for n, a in enumerate(pairs):
            line = lines[n]
            cleared = [jnp.where(within_turn, 0.0, v) for v in a]
            others = [b for b in range(blocks) if b not in (turn, ahead)]
            if ahead is not None:
                a[ahead] = cleared[ahead] - total_of([nexts[n][j] * spread_row(line, j) for j in range(SUB)])

            def placed(part):
                pads = [zero16] * blocks
                both = [part, zero8] if turn % 2 == 0 else [zero8, part]
                for side, chosen in ((0, low8), (1, ~low8)):
                    pads[side * blocks // 2 + turn // 2] = jnp.concatenate(
                        [jnp.where(chosen, v, 0.0) for v in both], axis=0
                    ).astype(jnp.bfloat16)
                return jnp.concatenate(pads, axis=0)

            high = line.astype(jnp.bfloat16).astype(jnp.float32)
            right = placed(high), placed(line - high)
            product = mm_split(split2(jnp.concatenate([a[b] for b in others], axis=0)), right)
            for number, b in enumerate(others):
                a[b] = cleared[b] - product[number * SUB : (number + 1) * SUB]
            a[turn] = line

    inverses = []
    for a, scale in zip(pairs, scales):
        both = jnp.concatenate(a, axis=0) * scale
        inverses.append(split2(jnp.concatenate([jnp.where(low64, both, 0.0), jnp.where(low64, 0.0, both)], axis=0)))
    def times(pair, first, last, parts):
        left = [v[first:last] for v in pair]
        return mm_split(left, [jnp.concatenate(p, axis=0) if len(p) > 1 else p[0] for p in zip(*parts)])

    zero = [jnp.zeros((half, LANES), jnp.bfloat16)] * 2
    wide = [jnp.zeros((half, own_rows), jnp.bfloat16)] * 2
    result = times(inverses[1], 0, LANES, (right_maps[1], right_maps[2]))
    maps_ref[0, 1] = result[0:half]
    maps_ref[0, 2] = result[half:]
    maps_ref[0, 3] = times(inverses[2], 0, half, (right_maps[3], zero))
    send(maps_ref.at[:, 1:], maps_out.at[:, 1:])
    interp_ref[...] = times(inverses[0], 0, half, (right_leaf, wide))
    send(interp_ref, interp_out)
    maps_ref[0, 0] = times(inverses[0], half, LANES, (zero, right_maps[0]))
    send(maps_ref.at[:, 0:1], maps_out.at[:, 0:1])
    for copy in copies:
        copy.wait()


def body(row_points, panel_points, test_vectors, leaf_skeleton, node_skeleton):
    devices = lax.axis_size("rows") * lax.axis_size("cols")
    vec_count, width = test_vectors.shape
    rows_here = row_points.shape[1]
    levels, skel = node_skeleton.shape[1:]
    packed, kept = pl.pallas_call(
        pack_kernel,
        out_shape=(
            pltpu.VMEM((devices, width + SUB, vec_count), jnp.bfloat16),
            pltpu.VMEM(row_points.shape, jnp.float32),
        ),
        in_specs=[VMEM] * 5,
        out_specs=(VMEM, VMEM),
        scratch_shapes=[pltpu.VMEM((SUB, LANES), jnp.float32)],
    )(row_points, panel_points, test_vectors.T, leaf_skeleton, node_skeleton)
    got = lax.all_to_all(packed, ("rows", "cols"), 0, 0, tiled=True)
    own_rows = rows_here // lax.axis_size("cols")
    lanes = 3 * LANES + own_rows
    block = min(devices, 2**levels * lax.axis_size("cols")) * width
    outs = (
        jax.ShapeDtypeStruct((skel, own_rows), jnp.float32),
        jax.ShapeDtypeStruct((1, levels, skel, 2 * skel), jnp.float32),
        jax.ShapeDtypeStruct((1, skel, 2 * vec_count), jnp.float32),
    )
    return pl.pallas_call(
        functools.partial(main_kernel, levels),
        out_shape=outs,
        in_specs=[VMEM] * 2,
        out_specs=tuple(pl.BlockSpec(memory_space=pl.ANY) for out in outs),
        scratch_shapes=[pltpu.VMEM(out.shape, out.dtype) for out in outs]
        + [
            pltpu.VMEM((block, LANES), jnp.bfloat16),
            pltpu.VMEM((block, lanes), jnp.bfloat16),
            pltpu.VMEM((block, lanes), jnp.bfloat16),
            pltpu.VMEM((2 * vec_count, lanes), jnp.float32),
            pltpu.SemaphoreType.DMA((4,)),
        ],
    )(pltpu.with_memory_space_constraint(got, pltpu.VMEM), pltpu.with_memory_space_constraint(kept, pltpu.VMEM))


def solution(mesh):
    placed = (
        P(None, "rows"),
        P(None, ("rows", "cols")),
        P(None, ("rows", "cols")),
        P("rows", None),
        P("rows", None, None),
    )
    return jax.shard_map(
        body,
        mesh=mesh,
        in_specs=placed,
        out_specs=(P(None, ("rows", "cols")), P("rows", None, None, None), P("rows", None, None)),
        check_vma=False,
    )
```

```python
import functools
import math

import jax
import jax.numpy as jnp
import numpy as np
from jax import lax
from jax.experimental import pallas as pl
from jax.experimental.pallas import tpu as pltpu
from jax.sharding import PartitionSpec as P

KAPPA = 40.0
SMOOTH = 0.05
RIDGE = 0.1
EPSILON = 1e-05

LANES = 128
SUB = 8
EXTRA = 4
VMEM = pl.BlockSpec(memory_space=pltpu.VMEM)

TURNS = KAPPA / (2 * math.pi)
SIN_POLY = (4.442867902871973, -7.30744341774541, 3.594788055359915, -0.7843739844598376)
COS_POLY = (1.4142134965650128, -6.978850988238946, 5.739461170681512, -1.8835629873012505, 0.31069819181076774)


def bf16_parts(value):
    parts = []
    for unused in range(3):
        parts.append(float(np.float32(value).astype(jnp.bfloat16)))
        value -= parts[-1]
    return parts


SCALE_PARTS = bf16_parts(TURNS * TURNS)


def iota(shape, dim):
    return lax.broadcasted_iota(jnp.int32, shape, dim)


def take_lanes(x, index):
    return jnp.take_along_axis(x, index, axis=1)


def swap_halves(x):
    return pltpu.roll(x, LANES // 2, axis=1)


def mm(a, b, dims=((1,), (0,)), precision=None):
    return lax.dot_general(a, b, (dims, ((), ())), precision=precision, preferred_element_type=jnp.float32)


def split2(x):
    high = x.astype(jnp.bfloat16)
    return high, (x - high.astype(jnp.float32)).astype(jnp.bfloat16)


def mm_split(a, b):
    (a_high, a_low), (b_high, b_low) = a, b
    return mm(jnp.concatenate([a_high, a_high, a_low], axis=1), jnp.concatenate([b_high, b_low, b_high], axis=0))


def split3(x):
    high = x.astype(jnp.bfloat16).astype(jnp.float32)
    rest = x - high
    mid = rest.astype(jnp.bfloat16).astype(jnp.float32)
    return high, mid, rest - mid


def pack_kernel(rows_ref, points_ref, vectors_ref, leaf_ref, node_ref, out_ref, kept_ref, stage):
    kept_ref[...] = rows_ref[...]
    width = vectors_ref.shape[0]
    half = LANES // 2
    low = iota((1, LANES), 1) < half
    stage[...] = jnp.zeros_like(stage)
    stage[0:1, 0:half] = leaf_ref[...].astype(jnp.float32)
    stage[1:5, 0:half] = node_ref[0].astype(jnp.float32)
    stage[5:8, 0:width] = points_ref[...].astype(jnp.float32)
    s = stage[...]
    index = s[0:1]
    index = (index + swap_halves(jnp.broadcast_to(index, (SUB, LANES)))[0:1]).astype(jnp.int32)
    index = jnp.broadcast_to(index, (SUB, LANES))
    stage[0:3, :] = rows_ref[:, 0:LANES]
    found = jnp.zeros((SUB, LANES), jnp.float32)
    for tile in range(rows_ref.shape[1] // LANES):
        stage[0:3, :] = rows_ref[:, tile * LANES : (tile + 1) * LANES]
        picked = take_lanes(stage[...], index & (LANES - 1))
        found = jnp.where(index // LANES == tile, picked, found)
    high, mid, tail = split3(found)
    swapped = swap_halves(s)
    points = s[5:6] + pltpu.roll(s, width, axis=1)[6:7] + pltpu.roll(s, 2 * width, axis=1)[7:8]
    halves = (
        [
            jnp.where(low, high[0:1], mid[0:1]),
            jnp.where(low, tail[0:1], high[1:2]),
            jnp.where(low, mid[1:2], tail[1:2]),
        ],
        [
            jnp.where(low, high[2:3], mid[2:3]),
            jnp.where(low, s[1:2], swapped[2:3]),
            jnp.where(low, s[3:4], swapped[4:5]),
        ],
    )
    column = lax.axis_index("cols")
    lines = [jnp.where(column == 0, a, b) for a, b in zip(*halves)]
    lines.append(jnp.where(low, points, tail[2:3]))
    block = jnp.concatenate([vectors_ref[...].astype(jnp.float32)] + lines, axis=0).astype(jnp.bfloat16)

    block = block.reshape(out_ref.shape[1:])

    def put(device, unused):
        out_ref[device] = block
        return unused

    lax.fori_loop(0, out_ref.shape[0], put, 0)


SETUP_PIECES = 4
STAGE_PIECES = 4
TURN_PIECES = (0, 0, 0, 0, 0, 0, 0, 0)
LEAF_TURN = 3


def evaluate(dist):
    inverse = lax.rsqrt(dist)
    turns = dist * inverse
    f = turns - jnp.round(turns)
    u = f * f
    scale = math.sqrt(TURNS)
    sine = SIN_POLY[-1] * scale
    cosine = COS_POLY[-1] * scale
    for value in SIN_POLY[-2::-1]:
        sine = sine * u + value * scale
    for value in COS_POLY[-2::-1]:
        cosine = cosine * u + value * scale
    sine = sine * f
    real = (TURNS - sine * sine) * inverse
    imag = (sine * cosine) * inverse
    return real.astype(jnp.bfloat16), imag.astype(jnp.bfloat16)


def main_kernel(levels, got_ref, rows_ref, interp_out, maps_out, top_out, interp_ref, maps_ref, top_ref, left_ref, kre_ref, kim_ref, samples_ref, sems):
    half = LANES // 2
    leaf = lax.axis_index("rows")
    column = lax.axis_index("cols")
    cols = lax.axis_size("cols")
    group_leaves = 2**levels
    group_devices = group_leaves * cols
    devices = got_ref.shape[0]
    width = (got_ref.shape[1] - 1) * EXTRA
    width_bits = width.bit_length() - 1
    lane8 = iota((SUB, LANES), 1)
    sub8 = iota((SUB, LANES), 0)
    low8 = lane8 < half
    member = leaf & (group_leaves - 1)
    mine = sub8 == member >> 1

    tree_lanes = 3 * LANES
    own_rows = rows_ref.shape[1] // cols
    start = pl.multiple_of(column * own_rows, LANES)
    own_points = rows_ref[:, pl.ds(start, own_rows)]

    def right_side(points):
        lanes = points[0].shape[1]
        lines = []
        norm = jnp.full((1, lanes), SMOOTH * SMOOTH, jnp.float32)
        for x in points:
            norm = norm + x * x
            lines += split3(x * (-2 * TURNS * TURNS))
        for repeat in range(6):
            lines += [jnp.full((1, lanes), v, jnp.float32) for v in SCALE_PARTS]
        lines += split3(norm * (TURNS * TURNS))
        lines.append(jnp.zeros((LANES - len(lines), lanes), jnp.float32))
        return jnp.concatenate(lines, axis=0).astype(jnp.bfloat16)

    block_devices = min(devices, group_devices)
    single = block_devices == devices
    block = block_devices * width
    vec_count = got_ref.shape[-1]
    eye = (iota((vec_count, vec_count), 0) == iota((vec_count, vec_count), 1)).astype(jnp.bfloat16)
    shape = (width, LANES)
    lane_of = iota(shape, 1)
    keep = (((lane_of ^ iota(shape, 0)) & (width - 1)) == 0) & (lane_of < 3 * width)
    ones = ((iota((1, LANES), 1) >= 27) & (iota((1, LANES), 1) < 30)).astype(jnp.float32)
    shape = (LANES, LANES)
    away = iota(shape, 1) - 3 * (iota(shape, 0) >> width_bits)
    within = iota(shape, 0) < 3 * width
    collect = jnp.concatenate(
        [(within & (away >= first) & (away < first + 3)).astype(jnp.bfloat16) for first in (0, 9, 18)], axis=0
    )

    def panel_vectors(number):
        got = got_ref[pl.ds(number * block_devices, block_devices), 0 : width // EXTRA].astype(jnp.float32)
        vectors = got.reshape(block, vec_count).astype(jnp.bfloat16)
        return mm(eye, vectors, dims=((1,), (1,))).astype(jnp.bfloat16)

    def panel_left(number):
        tail = got_ref[pl.ds(number * block_devices, block_devices), width // EXTRA].astype(jnp.float32)
        points = [jnp.where(keep, jnp.broadcast_to(tail[d, EXTRA - 1 : EXTRA], keep.shape), 0.0) for d in range(block_devices)]
        points = jnp.concatenate(points, axis=0)
        high, low = split2(points * points)
        left = mm(jnp.concatenate([points.astype(jnp.bfloat16), high, low], axis=1), collect) + ones
        left_ref[...] = left.astype(jnp.bfloat16)

    def fill(at, count, right, lane):
        dist = mm(left_ref[pl.ds(at, count), :], right)
        lanes = right.shape[1]
        kre_ref[pl.ds(at, count), lane : lane + lanes], kim_ref[pl.ds(at, count), lane : lane + lanes] = evaluate(dist)

    def sample(vectors, lane, lanes):
        both = [mm(vectors, k[:, lane : lane + lanes]) for k in (kre_ref, kim_ref)]
        return jnp.concatenate(both, axis=0)

    chunk = min(LANES, block)
    panel_left(0)
    right_own = right_side([own_points[c : c + 1] for c in range(3)])
    pieces = list(range(0, block, 16)) if single else []

    def own_pieces(count):
        for unused in range(min(count, len(pieces))):
            fill(pieces.pop(0), 16, right_own, tree_lanes)

    vectors = panel_vectors(0)
    group_start = (leaf // group_leaves) * group_devices
    extra = got_ref[pl.ds(group_start, group_devices), width // EXTRA].astype(jnp.float32)
    extra = extra.reshape(group_devices * EXTRA, LANES).astype(jnp.bfloat16)
    shape = (7 * 16, group_devices * EXTRA)
    at = iota(shape, 0)
    line = at >> 4
    place = jnp.where(line < 3, line, jnp.where(line == 3, EXTRA, jnp.where(line == 4, EXTRA - 1, line)))
    source = ((at & 7) * 2 + ((at >> 3) & 1)) * (cols * EXTRA) + place
    picked = mm((iota(shape, 1) == source).astype(jnp.bfloat16), extra)
    even = [picked[r * 16 : r * 16 + 8] for r in range(7)]
    odd = [picked[r * 16 + 8 : r * 16 + 16] for r in range(7)]
    even_s = [swap_halves(v) for v in even]
    odd_s = [swap_halves(v) for v in odd]
    coords = [
        jnp.where(low8, even[0] + even_s[0] + even[1], odd[0] + odd_s[0] + odd_s[1]),
        jnp.where(low8, even_s[1] + (even[2] + even_s[2]), odd[1] + (odd[2] + odd_s[2])),
        jnp.where(low8, even[3] + even_s[3] + even_s[4], odd[3] + odd_s[3] + odd[4]),
    ]
    lists = [
        jnp.where(low8, even[5], even_s[5]).astype(jnp.int32),
        jnp.where(low8, even_s[5], even[5]).astype(jnp.int32),
        jnp.where(low8, even[6], even_s[6]).astype(jnp.int32),
        jnp.where(low8, even_s[6], even[6]).astype(jnp.int32),
    ]

    def own_row(x):
        return jnp.sum(jnp.where(mine, x, jnp.zeros_like(x)), axis=0, keepdims=True)

    siblings = []
    own_lists = [own_row(lists[0])]
    stacked = coords
    for level in range(1, levels):
        own = [take_lanes(v, lists[level - 1]) for v in stacked]
        step = 2 ** (level - 1)
        upper = (sub8 & step) != 0
        other = [jnp.where(upper, pltpu.roll(v, step, axis=0), pltpu.roll(v, SUB - step, axis=0)) for v in own]
        siblings.append([own_row(v) for v in other])
        stacked = [jnp.where(low8 == upper, b, a) for a, b in zip(own, other)]
        own_lists.append(own_row(lists[level]))
        own_pieces(SETUP_PIECES)
    low1 = iota((1, LANES), 1) < half
    tiles = [[own_row(v) for v in coords]]
    tiles.append([jnp.where(low1, a, b) for a, b in zip(siblings[0], siblings[1])])
    tiles.append(siblings[2])
    right_tree = jnp.concatenate([right_side(t) for t in tiles], axis=1)

    for at in range(0, block, chunk):
        fill(at, chunk, right_tree, 0)
    samples_ref[:, 0:tree_lanes] = sample(vectors, 0, tree_lanes)
    if not single:
        for at in range(0, block, chunk):
            fill(at, chunk, right_own, tree_lanes)
        samples_ref[:, tree_lanes:] = sample(vectors, tree_lanes, own_rows)

        def more(number, unused):
            panel_left(number)
            for at in range(0, block, chunk):
                fill(at, chunk, right_tree, 0)
                fill(at, chunk, right_own, tree_lanes)
            samples_ref[...] += sample(panel_vectors(number), 0, tree_lanes + own_rows)
            return unused

        lax.fori_loop(1, devices // block_devices, more, 0)

    full = (2 * vec_count, LANES)
    low = iota(full, 1) < half
    pair0 = samples_ref[:, 0:LANES]
    pair0_s = swap_halves(pair0)
    pair12 = samples_ref[:, LANES : 2 * LANES]
    pair12_s = swap_halves(pair12)
    pair3 = samples_ref[:, 2 * LANES : 3 * LANES]

    def is_upper(level, shape):
        return (jnp.full(shape, member, jnp.int32) & 2**level) != 0

    upper0 = is_upper(0, full)
    stacks = [pair0]
    skels = [jnp.where(upper0 == low, pair0_s, pair0)]
    for level in range(levels):
        picked = take_lanes(stacks[level], jnp.broadcast_to(own_lists[level], full))
        skels.append(picked)
        own_pieces(STAGE_PIECES)
        if level + 1 < levels:
            up = is_upper(level + 1, full)
            if level == 0:
                other = jnp.where(up, pair12, pair12_s)
            elif level == 1:
                other = jnp.where(up, pair12_s, pair12)
            else:
                other = pair3
            stacks.append(jnp.where(low == up, other, picked))

    two = [jnp.where(low, skels[0], skels[1]).T, jnp.where(low, skels[2], skels[3]).T, skels[4].T]
    row_form = [two[0][0:half], two[0][half:], two[1][0:half], two[1][half:], two[2][0:half]]
    top_ref[0] = row_form[4]
    copies = []

    def send(source, target):
        copies.append(pltpu.make_async_copy(source, target, sems.at[len(copies)]))
        copies[-1].start()

    send(top_ref, top_out)
    row_form = [split2(v) for v in row_form]

    stacks = [split2(v) for v in stacks]
    square = (half, LANES)
    low64 = iota(square, 1) < half
    right_maps = [mm_split(row_form[level + 1], stacks[level]) for level in range(levels)]
    gram = mm_split(row_form[0], stacks[0])
    grams = [jnp.where(is_upper(0, square) == low64, swap_halves(gram), gram)]
    for level in range(levels):
        grams.append(take_lanes(right_maps[level], jnp.broadcast_to(own_lists[level], square)))
    pairs = []
    scales = []
    diagonal = iota(square, 0) == (iota(square, 1) & (half - 1))
    for a, b in ((0, 1), (2, 3), (4, 4)):
        gram = jnp.where(low64, grams[a], grams[b])
        trace = jnp.sum(jnp.where(diagonal, gram, 0.0), axis=0, keepdims=True)
        first = jnp.sum(jnp.where(low1, trace, 0.0), axis=1, keepdims=True)
        second = jnp.sum(jnp.where(low1, 0.0, trace), axis=1, keepdims=True)
        trace = jnp.where(low1, first, second)
        ridge = RIDGE * (2 * vec_count) * (trace * (1.0 / (half * 2 * vec_count)) + EPSILON)
        scales.append(RIDGE / ridge)
        gram = gram * scales[-1] + jnp.where(diagonal, RIDGE, 0.0)
        pairs.append([gram[r * SUB : (r + 1) * SUB] for r in range(half // SUB)])

    right_maps = [split2(v) for v in right_maps]
    where_in_half = lane8 & (half - 1)
    half_base = lane8 - where_in_half
    blocks = half // SUB

    def spread_row(x, row):
        return jnp.broadcast_to(x[row : row + 1], (SUB, LANES))

    def total_of(terms):
        while len(terms) > 1:
            terms = [x + y for x, y in zip(terms[::2], terms[1::2])]
        return terms[0]

    zero8 = jnp.zeros((SUB, LANES), jnp.float32)
    zero16 = jnp.zeros((2 * SUB, LANES), jnp.bfloat16)
    for turn in range(blocks):
        first = turn * SUB
        ahead = turn + 1 if turn + 1 < blocks else None
        within_turn = (where_in_half >> 3) == turn
        diagonals = [[take_lanes(a[turn], half_base + (first + j)) for j in range(SUB)] for a in pairs]
        if ahead is not None:
            nexts = [[take_lanes(a[ahead], half_base + (first + j)) for j in range(SUB)] for a in pairs]
        lines = [a[turn] for a in pairs]
        for s in range(SUB):
            own_pieces(TURN_PIECES[turn] if s % 2 == 0 else 0)
            here = where_in_half == first + s
            unit = jnp.where(sub8 == s, 1.0, 0.0)
            pivots = [spread_row(columns[s], s) for columns in diagonals]
            inverses = 1.0 / jnp.where(sub8 == 0, pivots[0], jnp.where(sub8 == 1, pivots[1], pivots[2]))
            for n in range(len(pairs)):
                columns = diagonals[n]
                inverse = spread_row(inverses, n)
                column = (columns[s] - unit) * inverse
                line = jnp.where(here, 1.0, spread_row(lines[n], s))
                lines[n] = jnp.where(here, unit, lines[n]) - column * line
                for j in range(s + 1, SUB):
                    columns[j] = columns[j] - column * spread_row(columns[j], s)
        if turn == LEAF_TURN:
            own_pieces(block)
            own_samples = sample(vectors, tree_lanes, own_rows) if single else samples_ref[:, tree_lanes:]
            right_leaf = split2(mm_split(row_form[0], split2(own_samples)))
        for n, a in enumerate(pairs):
            line = lines[n]
            cleared = [jnp.where(within_turn, 0.0, v) for v in a]
            others = [b for b in range(blocks) if b not in (turn, ahead)]
            if ahead is not None:
                a[ahead] = cleared[ahead] - total_of([nexts[n][j] * spread_row(line, j) for j in range(SUB)])

            def placed(part):
                pads = [zero16] * blocks
                both = [part, zero8] if turn % 2 == 0 else [zero8, part]
                for side, chosen in ((0, low8), (1, ~low8)):
                    pads[side * blocks // 2 + turn // 2] = jnp.concatenate(
                        [jnp.where(chosen, v, 0.0) for v in both], axis=0
                    ).astype(jnp.bfloat16)
                return jnp.concatenate(pads, axis=0)

            high = line.astype(jnp.bfloat16).astype(jnp.float32)
            right = placed(high), placed(line - high)
            product = mm_split(split2(jnp.concatenate([a[b] for b in others], axis=0)), right)
            for number, b in enumerate(others):
                a[b] = cleared[b] - product[number * SUB : (number + 1) * SUB]
            a[turn] = line

    inverses = []
    for a, scale in zip(pairs, scales):
        both = jnp.concatenate(a, axis=0) * scale
        inverses.append(split2(jnp.concatenate([jnp.where(low64, both, 0.0), jnp.where(low64, 0.0, both)], axis=0)))
    def times(pair, first, last, parts):
        left = [v[first:last] for v in pair]
        return mm_split(left, [jnp.concatenate(p, axis=0) if len(p) > 1 else p[0] for p in zip(*parts)])

    zero = [jnp.zeros((half, LANES), jnp.bfloat16)] * 2
    wide = [jnp.zeros((half, own_rows), jnp.bfloat16)] * 2
    result = times(inverses[1], 0, LANES, (right_maps[1], right_maps[2]))
    maps_ref[0, 1] = result[0:half]
    maps_ref[0, 2] = result[half:]
    maps_ref[0, 3] = times(inverses[2], 0, half, (right_maps[3], zero))
    send(maps_ref.at[:, 1:], maps_out.at[:, 1:])
    interp_ref[...] = times(inverses[0], 0, half, (right_leaf, wide))
    send(interp_ref, interp_out)
    maps_ref[0, 0] = times(inverses[0], half, LANES, (zero, right_maps[0]))
    send(maps_ref.at[:, 0:1], maps_out.at[:, 0:1])
    for copy in copies:
        copy.wait()


def body(row_points, panel_points, test_vectors, leaf_skeleton, node_skeleton):
    devices = lax.axis_size("rows") * lax.axis_size("cols")
    vec_count, width = test_vectors.shape
    rows_here = row_points.shape[1]
    levels, skel = node_skeleton.shape[1:]
    packed, kept = pl.pallas_call(
        pack_kernel,
        out_shape=(
            pltpu.VMEM((devices, width // EXTRA + 1, EXTRA, vec_count), jnp.bfloat16),
            pltpu.VMEM(row_points.shape, jnp.float32),
        ),
        in_specs=[VMEM] * 5,
        out_specs=(VMEM, VMEM),
        scratch_shapes=[pltpu.VMEM((SUB, LANES), jnp.float32)],
    )(row_points, panel_points, test_vectors.T, leaf_skeleton, node_skeleton)
    got = lax.all_to_all(packed, ("rows", "cols"), 0, 0, tiled=True)
    own_rows = rows_here // lax.axis_size("cols")
    lanes = 3 * LANES + own_rows
    block = min(devices, 2**levels * lax.axis_size("cols")) * width
    outs = (
        jax.ShapeDtypeStruct((skel, own_rows), jnp.float32),
        jax.ShapeDtypeStruct((1, levels, skel, 2 * skel), jnp.float32),
        jax.ShapeDtypeStruct((1, skel, 2 * vec_count), jnp.float32),
    )
    return pl.pallas_call(
        functools.partial(main_kernel, levels),
        out_shape=outs,
        in_specs=[VMEM] * 2,
        out_specs=tuple(pl.BlockSpec(memory_space=pl.ANY) for out in outs),
        scratch_shapes=[pltpu.VMEM(out.shape, out.dtype) for out in outs]
        + [
            pltpu.VMEM((block, LANES), jnp.bfloat16),
            pltpu.VMEM((block, lanes), jnp.bfloat16),
            pltpu.VMEM((block, lanes), jnp.bfloat16),
            pltpu.VMEM((2 * vec_count, lanes), jnp.float32),
            pltpu.SemaphoreType.DMA((4,)),
        ],
    )(pltpu.with_memory_space_constraint(got, pltpu.VMEM), pltpu.with_memory_space_constraint(kept, pltpu.VMEM))


def solution(mesh):
    placed = (
        P(None, "rows"),
        P(None, ("rows", "cols")),
        P(None, ("rows", "cols")),
        P("rows", None),
        P("rows", None, None),
    )
    return jax.shard_map(
        body,
        mesh=mesh,
        in_specs=placed,
        out_specs=(P(None, ("rows", "cols")), P("rows", None, None, None), P("rows", None, None)),
        check_vma=False,
    )
```

```python
import functools
import math

import jax
import jax.numpy as jnp
import numpy as np
from jax import lax
from jax.experimental import pallas as pl
from jax.experimental.pallas import tpu as pltpu
from jax.sharding import PartitionSpec as P

KAPPA = 40.0
SMOOTH = 0.05
RIDGE = 0.1
EPSILON = 1e-05

LANES = 128
SUB = 8
EXTRA = 4
VMEM = pl.BlockSpec(memory_space=pltpu.VMEM)

TURNS = KAPPA / (2 * math.pi)
SIN_POLY = (4.442867902871973, -7.30744341774541, 3.594788055359915, -0.7843739844598376)
COS_POLY = (1.4142134965650128, -6.978850988238946, 5.739461170681512, -1.8835629873012505, 0.31069819181076774)


def bf16_parts(value):
    parts = []
    for unused in range(3):
        parts.append(float(np.float32(value).astype(jnp.bfloat16)))
        value -= parts[-1]
    return parts


SCALE_PARTS = bf16_parts(TURNS * TURNS)


def iota(shape, dim):
    return lax.broadcasted_iota(jnp.int32, shape, dim)


def take_lanes(x, index):
    return jnp.take_along_axis(x, index, axis=1)


def swap_halves(x):
    return pltpu.roll(x, LANES // 2, axis=1)


def mm(a, b, dims=((1,), (0,)), precision=None):
    return lax.dot_general(a, b, (dims, ((), ())), precision=precision, preferred_element_type=jnp.float32)


def split2(x):
    high = x.astype(jnp.bfloat16)
    return high, (x - high.astype(jnp.float32)).astype(jnp.bfloat16)


def mm_split(a, b):
    rows, lanes = a[0].shape[0], b[0].shape[1]
    out = mm(jnp.concatenate(a, axis=0), jnp.concatenate(b, axis=1))
    return out[:rows, :lanes] + (out[:rows, lanes:] + out[rows:, :lanes])


def split3(x):
    high = x.astype(jnp.bfloat16).astype(jnp.float32)
    rest = x - high
    mid = rest.astype(jnp.bfloat16).astype(jnp.float32)
    return high, mid, rest - mid


def pack_kernel(rows_ref, points_ref, vectors_ref, leaf_ref, node_ref, out_ref, kept_ref, stage):
    kept_ref[...] = rows_ref[...]
    width = vectors_ref.shape[0]
    half = LANES // 2
    low = iota((1, LANES), 1) < half
    stage[...] = jnp.zeros_like(stage)
    stage[0:1, 0:half] = leaf_ref[...].astype(jnp.float32)
    stage[1:5, 0:half] = node_ref[0].astype(jnp.float32)
    stage[5:8, 0:width] = points_ref[...].astype(jnp.float32)
    s = stage[...]
    index = s[0:1]
    index = (index + swap_halves(jnp.broadcast_to(index, (SUB, LANES)))[0:1]).astype(jnp.int32)
    index = jnp.broadcast_to(index, (SUB, LANES))
    stage[0:3, :] = rows_ref[:, 0:LANES]
    found = jnp.zeros((SUB, LANES), jnp.float32)
    for tile in range(rows_ref.shape[1] // LANES):
        stage[0:3, :] = rows_ref[:, tile * LANES : (tile + 1) * LANES]
        picked = take_lanes(stage[...], index & (LANES - 1))
        found = jnp.where(index // LANES == tile, picked, found)
    high, mid, tail = split3(found)
    swapped = swap_halves(s)
    points = s[5:6] + pltpu.roll(s, width, axis=1)[6:7] + pltpu.roll(s, 2 * width, axis=1)[7:8]
    halves = (
        [
            jnp.where(low, high[0:1], mid[0:1]),
            jnp.where(low, tail[0:1], high[1:2]),
            jnp.where(low, mid[1:2], tail[1:2]),
        ],
        [
            jnp.where(low, high[2:3], mid[2:3]),
            jnp.where(low, s[1:2], swapped[2:3]),
            jnp.where(low, s[3:4], swapped[4:5]),
        ],
    )
    column = lax.axis_index("cols")
    lines = [jnp.where(column == 0, a, b) for a, b in zip(*halves)]
    lines.append(jnp.where(low, points, tail[2:3]))
    block = jnp.concatenate([vectors_ref[...].astype(jnp.float32)] + lines, axis=0).astype(jnp.bfloat16)

    block = block.reshape(out_ref.shape[1:])

    def put(device, unused):
        out_ref[device] = block
        return unused

    lax.fori_loop(0, out_ref.shape[0], put, 0)


STAGE_PIECES = 8
TURN_PIECES = (0, 0, 0, 0, 0, 0, 0, 0)
LEAF_TURN = 3


def evaluate(dist):
    inverse = lax.rsqrt(dist)
    turns = dist * inverse
    f = turns - jnp.round(turns)
    u = f * f
    scale = math.sqrt(TURNS)
    sine = SIN_POLY[-1] * scale
    cosine = COS_POLY[-1] * scale
    for value in SIN_POLY[-2::-1]:
        sine = sine * u + value * scale
    for value in COS_POLY[-2::-1]:
        cosine = cosine * u + value * scale
    sine = sine * f
    real = (TURNS - sine * sine) * inverse
    imag = (sine * cosine) * inverse
    return real.astype(jnp.bfloat16), imag.astype(jnp.bfloat16)


def main_kernel(levels, got_ref, rows_ref, interp_out, maps_out, top_out, interp_ref, maps_ref, top_ref, left_ref, kre_ref, kim_ref, samples_ref, sems):
    half = LANES // 2
    leaf = lax.axis_index("rows")
    column = lax.axis_index("cols")
    cols = lax.axis_size("cols")
    group_leaves = 2**levels
    group_devices = group_leaves * cols
    devices = got_ref.shape[0]
    width = (got_ref.shape[1] - 1) * EXTRA
    width_bits = width.bit_length() - 1
    lane8 = iota((SUB, LANES), 1)
    sub8 = iota((SUB, LANES), 0)
    low8 = lane8 < half
    member = leaf & (group_leaves - 1)
    mine = sub8 == member >> 1

    tree_lanes = 3 * LANES
    own_rows = rows_ref.shape[1] // cols
    start = pl.multiple_of(column * own_rows, LANES)
    own_points = rows_ref[:, pl.ds(start, own_rows)]

    def right_side(points):
        lanes = points[0].shape[1]
        lines = []
        norm = jnp.full((1, lanes), SMOOTH * SMOOTH, jnp.float32)
        for x in points:
            norm = norm + x * x
            lines += split3(x * (-2 * TURNS * TURNS))
        for repeat in range(6):
            lines += [jnp.full((1, lanes), v, jnp.float32) for v in SCALE_PARTS]
        lines += split3(norm * (TURNS * TURNS))
        lines.append(jnp.zeros((LANES - len(lines), lanes), jnp.float32))
        return jnp.concatenate(lines, axis=0).astype(jnp.bfloat16)

    block_devices = min(devices, group_devices)
    single = block_devices == devices
    block = block_devices * width
    vec_count = got_ref.shape[-1]
    eye = (iota((vec_count, vec_count), 0) == iota((vec_count, vec_count), 1)).astype(jnp.bfloat16)
    shape = (width, LANES)
    lane_of = iota(shape, 1)
    keep = (((lane_of ^ iota(shape, 0)) & (width - 1)) == 0) & (lane_of < 3 * width)
    ones = ((iota((1, LANES), 1) >= 27) & (iota((1, LANES), 1) < 30)).astype(jnp.float32)
    shape = (LANES, LANES)
    away = iota(shape, 1) - 3 * (iota(shape, 0) >> width_bits)
    within = iota(shape, 0) < 3 * width
    collect = jnp.concatenate(
        [(within & (away >= first) & (away < first + 3)).astype(jnp.bfloat16) for first in (0, 9, 18)], axis=0
    )

    def panel_vectors(number):
        got = got_ref[pl.ds(number * block_devices, block_devices), 0 : width // EXTRA].astype(jnp.float32)
        vectors = got.reshape(block, vec_count).astype(jnp.bfloat16)
        return mm(eye, vectors, dims=((1,), (1,))).astype(jnp.bfloat16)

    def panel_left(number):
        tail = got_ref[pl.ds(number * block_devices, block_devices), width // EXTRA].astype(jnp.float32)
        points = [jnp.where(keep, jnp.broadcast_to(tail[d, EXTRA - 1 : EXTRA], keep.shape), 0.0) for d in range(block_devices)]
        points = jnp.concatenate(points, axis=0)
        high, low = split2(points * points)
        left = mm(jnp.concatenate([points.astype(jnp.bfloat16), high, low], axis=1), collect) + ones
        left_ref[...] = left.astype(jnp.bfloat16)

    def fill(at, count, right, lane):
        dist = mm(left_ref[pl.ds(at, count), :], right)
        lanes = right.shape[1]
        kre_ref[pl.ds(at, count), lane : lane + lanes], kim_ref[pl.ds(at, count), lane : lane + lanes] = evaluate(dist)

    def sample(vectors, lane, lanes):
        both = [mm(vectors, k[:, lane : lane + lanes]) for k in (kre_ref, kim_ref)]
        return jnp.concatenate(both, axis=0)

    group_start = (leaf // group_leaves) * group_devices
    extra = got_ref[pl.ds(group_start, group_devices), width // EXTRA].astype(jnp.float32)
    extra = extra.reshape(group_devices * EXTRA, LANES).astype(jnp.bfloat16)
    shape = (7 * 16, group_devices * EXTRA)
    at = iota(shape, 0)
    line = at >> 4
    place = jnp.where(line < 3, line, jnp.where(line == 3, EXTRA, jnp.where(line == 4, EXTRA - 1, line)))
    source = ((at & 7) * 2 + ((at >> 3) & 1)) * (cols * EXTRA) + place
    picked = mm((iota(shape, 1) == source).astype(jnp.bfloat16), extra)
    even = [picked[r * 16 : r * 16 + 8] for r in range(7)]
    odd = [picked[r * 16 + 8 : r * 16 + 16] for r in range(7)]
    even_s = [swap_halves(v) for v in even]
    odd_s = [swap_halves(v) for v in odd]
    coords = [
        jnp.where(low8, even[0] + even_s[0] + even[1], odd[0] + odd_s[0] + odd_s[1]),
        jnp.where(low8, even_s[1] + (even[2] + even_s[2]), odd[1] + (odd[2] + odd_s[2])),
        jnp.where(low8, even[3] + even_s[3] + even_s[4], odd[3] + odd_s[3] + odd[4]),
    ]
    lists = [
        jnp.where(low8, even[5], even_s[5]).astype(jnp.int32),
        jnp.where(low8, even_s[5], even[5]).astype(jnp.int32),
        jnp.where(low8, even[6], even_s[6]).astype(jnp.int32),
        jnp.where(low8, even_s[6], even[6]).astype(jnp.int32),
    ]

    def own_row(x):
        return jnp.sum(jnp.where(mine, x, jnp.zeros_like(x)), axis=0, keepdims=True)

    siblings = []
    own_lists = [own_row(lists[0])]
    stacked = coords
    for level in range(1, levels):
        own = [take_lanes(v, lists[level - 1]) for v in stacked]
        step = 2 ** (level - 1)
        upper = (sub8 & step) != 0
        other = [jnp.where(upper, pltpu.roll(v, step, axis=0), pltpu.roll(v, SUB - step, axis=0)) for v in own]
        siblings.append([own_row(v) for v in other])
        stacked = [jnp.where(low8 == upper, b, a) for a, b in zip(own, other)]
        own_lists.append(own_row(lists[level]))
    low1 = iota((1, LANES), 1) < half
    tiles = [[own_row(v) for v in coords]]
    tiles.append([jnp.where(low1, a, b) for a, b in zip(siblings[0], siblings[1])])
    tiles.append(siblings[2])
    chunk = min(LANES, block)
    panel_left(0)
    right_own = right_side([own_points[c : c + 1] for c in range(3)])
    pieces = list(range(0, block, 16)) if single else []

    def own_pieces(count):
        for unused in range(min(count, len(pieces))):
            fill(pieces.pop(0), 16, right_own, tree_lanes)

    vectors = panel_vectors(0)
    right_tree = jnp.concatenate([right_side(t) for t in tiles], axis=1)

    for at in range(0, block, chunk):
        fill(at, chunk, right_tree, 0)
    samples_ref[:, 0:tree_lanes] = sample(vectors, 0, tree_lanes)
    if not single:
        for at in range(0, block, chunk):
            fill(at, chunk, right_own, tree_lanes)
        samples_ref[:, tree_lanes:] = sample(vectors, tree_lanes, own_rows)

        def more(number, unused):
            panel_left(number)
            for at in range(0, block, chunk):
                fill(at, chunk, right_tree, 0)
                fill(at, chunk, right_own, tree_lanes)
            samples_ref[...] += sample(panel_vectors(number), 0, tree_lanes + own_rows)
            return unused

        lax.fori_loop(1, devices // block_devices, more, 0)

    full = (2 * vec_count, LANES)
    low = iota(full, 1) < half
    pair0 = samples_ref[:, 0:LANES]
    pair0_s = swap_halves(pair0)
    pair12 = samples_ref[:, LANES : 2 * LANES]
    pair12_s = swap_halves(pair12)
    pair3 = samples_ref[:, 2 * LANES : 3 * LANES]

    def is_upper(level, shape):
        return (jnp.full(shape, member, jnp.int32) & 2**level) != 0

    upper0 = is_upper(0, full)
    stacks = [pair0]
    skels = [jnp.where(upper0 == low, pair0_s, pair0)]
    for level in range(levels):
        picked = take_lanes(stacks[level], jnp.broadcast_to(own_lists[level], full))
        skels.append(picked)
        own_pieces(STAGE_PIECES)
        if level + 1 < levels:
            up = is_upper(level + 1, full)
            if level == 0:
                other = jnp.where(up, pair12, pair12_s)
            elif level == 1:
                other = jnp.where(up, pair12_s, pair12)
            else:
                other = pair3
            stacks.append(jnp.where(low == up, other, picked))

    two = [jnp.where(low, skels[0], skels[1]).T, jnp.where(low, skels[2], skels[3]).T, skels[4].T]
    row_form = [two[0][0:half], two[0][half:], two[1][0:half], two[1][half:], two[2][0:half]]
    top_ref[0] = row_form[4]
    copies = []

    def send(source, target):
        copies.append(pltpu.make_async_copy(source, target, sems.at[len(copies)]))
        copies[-1].start()

    send(top_ref, top_out)
    row_form = [split2(v) for v in row_form]

    stacks = [split2(v) for v in stacks]
    square = (half, LANES)
    low64 = iota(square, 1) < half
    right_maps = [mm_split(row_form[level + 1], stacks[level]) for level in range(levels)]
    gram = mm_split(row_form[0], stacks[0])
    grams = [jnp.where(is_upper(0, square) == low64, swap_halves(gram), gram)]
    for level in range(levels):
        grams.append(take_lanes(right_maps[level], jnp.broadcast_to(own_lists[level], square)))
    pairs = []
    scales = []
    diagonal = iota(square, 0) == (iota(square, 1) & (half - 1))
    for a, b in ((0, 1), (2, 3), (4, 4)):
        gram = jnp.where(low64, grams[a], grams[b])
        trace = jnp.sum(jnp.where(diagonal, gram, 0.0), axis=0, keepdims=True)
        first = jnp.sum(jnp.where(low1, trace, 0.0), axis=1, keepdims=True)
        second = jnp.sum(jnp.where(low1, 0.0, trace), axis=1, keepdims=True)
        trace = jnp.where(low1, first, second)
        ridge = RIDGE * (2 * vec_count) * (trace * (1.0 / (half * 2 * vec_count)) + EPSILON)
        scales.append(RIDGE / ridge)
        gram = gram * scales[-1] + jnp.where(diagonal, RIDGE, 0.0)
        pairs.append([gram[r * SUB : (r + 1) * SUB] for r in range(half // SUB)])

    right_maps = [split2(v) for v in right_maps]
    where_in_half = lane8 & (half - 1)
    half_base = lane8 - where_in_half
    blocks = half // SUB

    def spread_row(x, row):
        return jnp.broadcast_to(x[row : row + 1], (SUB, LANES))

    def total_of(terms):
        while len(terms) > 1:
            terms = [x + y for x, y in zip(terms[::2], terms[1::2])]
        return terms[0]

    zero8 = jnp.zeros((SUB, LANES), jnp.float32)
    zero16 = jnp.zeros((2 * SUB, LANES), jnp.bfloat16)
    for turn in range(blocks):
        first = turn * SUB
        ahead = turn + 1 if turn + 1 < blocks else None
        within_turn = (where_in_half >> 3) == turn
        diagonals = [[take_lanes(a[turn], half_base + (first + j)) for j in range(SUB)] for a in pairs]
        if ahead is not None:
            nexts = [[take_lanes(a[ahead], half_base + (first + j)) for j in range(SUB)] for a in pairs]
        lines = [a[turn] for a in pairs]
        for s in range(SUB):
            own_pieces(TURN_PIECES[turn] if s % 2 == 0 else 0)
            here = where_in_half == first + s
            unit = jnp.where(sub8 == s, 1.0, 0.0)
            pivots = [spread_row(columns[s], s) for columns in diagonals]
            inverses = 1.0 / jnp.where(sub8 == 0, pivots[0], jnp.where(sub8 == 1, pivots[1], pivots[2]))
            for n in range(len(pairs)):
                columns = diagonals[n]
                inverse = spread_row(inverses, n)
                column = (columns[s] - unit) * inverse
                line = jnp.where(here, 1.0, spread_row(lines[n], s))
                lines[n] = jnp.where(here, unit, lines[n]) - column * line
                for j in range(s + 1, SUB):
                    columns[j] = columns[j] - column * spread_row(columns[j], s)
        if turn == LEAF_TURN:
            own_pieces(block)
            own_samples = sample(vectors, tree_lanes, own_rows) if single else samples_ref[:, tree_lanes:]
            right_leaf = split2(mm_split(row_form[0], split2(own_samples)))
        for n, a in enumerate(pairs):
            line = lines[n]
            cleared = [jnp.where(within_turn, 0.0, v) for v in a]
            others = [b for b in range(blocks) if b not in (turn, ahead)]
            if ahead is not None:
                a[ahead] = cleared[ahead] - total_of([nexts[n][j] * spread_row(line, j) for j in range(SUB)])

            def placed(part):
                pads = [zero16] * blocks
                both = [part, zero8] if turn % 2 == 0 else [zero8, part]
                for side, chosen in ((0, low8), (1, ~low8)):
                    pads[side * blocks // 2 + turn // 2] = jnp.concatenate(
                        [jnp.where(chosen, v, 0.0) for v in both], axis=0
                    ).astype(jnp.bfloat16)
                return jnp.concatenate(pads, axis=0)

            high = line.astype(jnp.bfloat16).astype(jnp.float32)
            right = placed(high), placed(line - high)
            padded = others + [turn] * (len(others) % 2)
            product = mm_split(split2(jnp.concatenate([a[b] for b in padded], axis=0)), right)
            for number, b in enumerate(others):
                a[b] = cleared[b] - product[number * SUB : (number + 1) * SUB]
            a[turn] = line

    inverses = []
    for a, scale in zip(pairs, scales):
        both = jnp.concatenate(a, axis=0) * scale
        inverses.append(split2(jnp.concatenate([jnp.where(low64, both, 0.0), jnp.where(low64, 0.0, both)], axis=0)))
    def times(pair, first, last, parts):
        left = [v[first:last] for v in pair]
        return mm_split(left, [jnp.concatenate(p, axis=0) if len(p) > 1 else p[0] for p in zip(*parts)])

    zero = [jnp.zeros((half, LANES), jnp.bfloat16)] * 2
    wide = [jnp.zeros((half, own_rows), jnp.bfloat16)] * 2
    result = times(inverses[1], 0, LANES, (right_maps[1], right_maps[2]))
    maps_ref[0, 1] = result[0:half]
    maps_ref[0, 2] = result[half:]
    maps_ref[0, 3] = times(inverses[2], 0, half, (right_maps[3], zero))
    send(maps_ref.at[:, 1:], maps_out.at[:, 1:])
    interp_ref[...] = times(inverses[0], 0, half, (right_leaf, wide))
    send(interp_ref, interp_out)
    maps_ref[0, 0] = times(inverses[0], half, LANES, (zero, right_maps[0]))
    send(maps_ref.at[:, 0:1], maps_out.at[:, 0:1])
    for copy in copies:
        copy.wait()


def body(row_points, panel_points, test_vectors, leaf_skeleton, node_skeleton):
    devices = lax.axis_size("rows") * lax.axis_size("cols")
    vec_count, width = test_vectors.shape
    rows_here = row_points.shape[1]
    levels, skel = node_skeleton.shape[1:]
    packed, kept = pl.pallas_call(
        pack_kernel,
        out_shape=(
            pltpu.VMEM((devices, width // EXTRA + 1, EXTRA, vec_count), jnp.bfloat16),
            pltpu.VMEM(row_points.shape, jnp.float32),
        ),
        in_specs=[VMEM] * 5,
        out_specs=(VMEM, VMEM),
        scratch_shapes=[pltpu.VMEM((SUB, LANES), jnp.float32)],
    )(row_points, panel_points, test_vectors.T, leaf_skeleton, node_skeleton)
    got = lax.all_to_all(packed, ("rows", "cols"), 0, 0, tiled=True)
    own_rows = rows_here // lax.axis_size("cols")
    lanes = 3 * LANES + own_rows
    block = min(devices, 2**levels * lax.axis_size("cols")) * width
    outs = (
        jax.ShapeDtypeStruct((skel, own_rows), jnp.float32),
        jax.ShapeDtypeStruct((1, levels, skel, 2 * skel), jnp.float32),
        jax.ShapeDtypeStruct((1, skel, 2 * vec_count), jnp.float32),
    )
    return pl.pallas_call(
        functools.partial(main_kernel, levels),
        out_shape=outs,
        in_specs=[VMEM] * 2,
        out_specs=tuple(pl.BlockSpec(memory_space=pl.ANY) for out in outs),
        scratch_shapes=[pltpu.VMEM(out.shape, out.dtype) for out in outs]
        + [
            pltpu.VMEM((block, LANES), jnp.bfloat16),
            pltpu.VMEM((block, lanes), jnp.bfloat16),
            pltpu.VMEM((block, lanes), jnp.bfloat16),
            pltpu.VMEM((2 * vec_count, lanes), jnp.float32),
            pltpu.SemaphoreType.DMA((4,)),
        ],
    )(pltpu.with_memory_space_constraint(got, pltpu.VMEM), pltpu.with_memory_space_constraint(kept, pltpu.VMEM))


def solution(mesh):
    placed = (
        P(None, "rows"),
        P(None, ("rows", "cols")),
        P(None, ("rows", "cols")),
        P("rows", None),
        P("rows", None, None),
    )
    return jax.shard_map(
        body,
        mesh=mesh,
        in_specs=placed,
        out_specs=(P(None, ("rows", "cols")), P("rows", None, None, None), P("rows", None, None)),
        check_vma=False,
    )
```

```python
import functools
import math

import jax
import jax.numpy as jnp
import numpy as np
from jax import lax
from jax.experimental import pallas as pl
from jax.experimental.pallas import tpu as pltpu
from jax.sharding import PartitionSpec as P

KAPPA = 40.0
SMOOTH = 0.05
RIDGE = 0.1
EPSILON = 1e-05

LANES = 128
SUB = 8
EXTRA = 4
VMEM = pl.BlockSpec(memory_space=pltpu.VMEM)

TURNS = KAPPA / (2 * math.pi)
SIN_POLY = (4.442867902871973, -7.30744341774541, 3.594788055359915, -0.7843739844598376)
COS_POLY = (1.4142134965650128, -6.978850988238946, 5.739461170681512, -1.8835629873012505, 0.31069819181076774)


def bf16_parts(value):
    parts = []
    for unused in range(3):
        parts.append(float(np.float32(value).astype(jnp.bfloat16)))
        value -= parts[-1]
    return parts


SCALE_PARTS = bf16_parts(TURNS * TURNS)


def iota(shape, dim):
    return lax.broadcasted_iota(jnp.int32, shape, dim)


def take_lanes(x, index):
    return jnp.take_along_axis(x, index, axis=1)


def swap_halves(x):
    return pltpu.roll(x, LANES // 2, axis=1)


def mm(a, b, dims=((1,), (0,)), precision=None):
    return lax.dot_general(a, b, (dims, ((), ())), precision=precision, preferred_element_type=jnp.float32)


def split2(x):
    high = x.astype(jnp.bfloat16)
    return high, (x - high.astype(jnp.float32)).astype(jnp.bfloat16)


def mm_split(a, b):
    rows, lanes = a[0].shape[0], b[0].shape[1]
    out = mm(jnp.concatenate(a, axis=0), jnp.concatenate(b, axis=1))
    return out[:rows, :lanes] + (out[:rows, lanes:] + out[rows:, :lanes])


def split3(x):
    high = x.astype(jnp.bfloat16).astype(jnp.float32)
    rest = x - high
    mid = rest.astype(jnp.bfloat16).astype(jnp.float32)
    return high, mid, rest - mid


def pack_kernel(rows_ref, points_ref, vectors_ref, leaf_ref, node_ref, out_ref, kept_ref, stage):
    kept_ref[...] = rows_ref[...]
    width = vectors_ref.shape[0]
    half = LANES // 2
    low = iota((1, LANES), 1) < half
    stage[...] = jnp.zeros_like(stage)
    stage[0:1, 0:half] = leaf_ref[...].astype(jnp.float32)
    stage[1:5, 0:half] = node_ref[0].astype(jnp.float32)
    stage[5:8, 0:width] = points_ref[...].astype(jnp.float32)
    s = stage[...]
    index = s[0:1]
    index = (index + swap_halves(jnp.broadcast_to(index, (SUB, LANES)))[0:1]).astype(jnp.int32)
    index = jnp.broadcast_to(index, (SUB, LANES))
    stage[0:3, :] = rows_ref[:, 0:LANES]
    found = jnp.zeros((SUB, LANES), jnp.float32)
    for tile in range(rows_ref.shape[1] // LANES):
        stage[0:3, :] = rows_ref[:, tile * LANES : (tile + 1) * LANES]
        picked = take_lanes(stage[...], index & (LANES - 1))
        found = jnp.where(index // LANES == tile, picked, found)
    high, mid, tail = split3(found)
    swapped = swap_halves(s)
    points = s[5:6] + pltpu.roll(s, width, axis=1)[6:7] + pltpu.roll(s, 2 * width, axis=1)[7:8]
    halves = (
        [
            jnp.where(low, high[0:1], mid[0:1]),
            jnp.where(low, tail[0:1], high[1:2]),
            jnp.where(low, mid[1:2], tail[1:2]),
        ],
        [
            jnp.where(low, high[2:3], mid[2:3]),
            jnp.where(low, s[1:2], swapped[2:3]),
            jnp.where(low, s[3:4], swapped[4:5]),
        ],
    )
    column = lax.axis_index("cols")
    lines = [jnp.where(column == 0, a, b) for a, b in zip(*halves)]
    lines.append(jnp.where(low, points, tail[2:3]))
    block = jnp.concatenate([vectors_ref[...].astype(jnp.float32)] + lines, axis=0).astype(jnp.bfloat16)

    block = block.reshape(out_ref.shape[1:])

    def put(device, unused):
        out_ref[device] = block
        return unused

    lax.fori_loop(0, out_ref.shape[0], put, 0, unroll=8)


STAGE_PIECES = 8
TURN_PIECES = (0, 0, 0, 0, 0, 0, 0, 0)
LEAF_TURN = 3


def evaluate(dist):
    inverse = lax.rsqrt(dist)
    turns = dist * inverse
    f = turns - jnp.round(turns)
    u = f * f
    scale = math.sqrt(TURNS)
    sine = SIN_POLY[-1] * scale
    cosine = COS_POLY[-1] * scale
    for value in SIN_POLY[-2::-1]:
        sine = sine * u + value * scale
    for value in COS_POLY[-2::-1]:
        cosine = cosine * u + value * scale
    sine = sine * f
    real = (TURNS - sine * sine) * inverse
    imag = (sine * cosine) * inverse
    return real.astype(jnp.bfloat16), imag.astype(jnp.bfloat16)


def main_kernel(levels, got_ref, rows_ref, interp_out, maps_out, top_out, interp_ref, maps_ref, top_ref, left_ref, kre_ref, kim_ref, samples_ref, sems):
    half = LANES // 2
    leaf = lax.axis_index("rows")
    column = lax.axis_index("cols")
    cols = lax.axis_size("cols")
    group_leaves = 2**levels
    group_devices = group_leaves * cols
    devices = got_ref.shape[0]
    width = (got_ref.shape[1] - 1) * EXTRA
    width_bits = width.bit_length() - 1
    lane8 = iota((SUB, LANES), 1)
    sub8 = iota((SUB, LANES), 0)
    low8 = lane8 < half
    member = leaf & (group_leaves - 1)
    mine = sub8 == member >> 1

    tree_lanes = 3 * LANES
    own_rows = rows_ref.shape[1] // cols
    start = pl.multiple_of(column * own_rows, LANES)
    own_points = rows_ref[:, pl.ds(start, own_rows)]

    def right_side(points):
        lanes = points[0].shape[1]
        lines = []
        norm = jnp.full((1, lanes), SMOOTH * SMOOTH, jnp.float32)
        for x in points:
            norm = norm + x * x
            lines += split3(x * (-2 * TURNS * TURNS))
        for repeat in range(6):
            lines += [jnp.full((1, lanes), v, jnp.float32) for v in SCALE_PARTS]
        lines += split3(norm * (TURNS * TURNS))
        lines.append(jnp.zeros((LANES - len(lines), lanes), jnp.float32))
        return jnp.concatenate(lines, axis=0).astype(jnp.bfloat16)

    block_devices = min(devices, group_devices)
    single = block_devices == devices
    block = block_devices * width
    vec_count = got_ref.shape[-1]
    eye = (iota((vec_count, vec_count), 0) == iota((vec_count, vec_count), 1)).astype(jnp.bfloat16)
    shape = (width, LANES)
    lane_of = iota(shape, 1)
    keep = (((lane_of ^ iota(shape, 0)) & (width - 1)) == 0) & (lane_of < 3 * width)
    ones = ((iota((1, LANES), 1) >= 27) & (iota((1, LANES), 1) < 30)).astype(jnp.float32)
    shape = (LANES, LANES)
    away = iota(shape, 1) - 3 * (iota(shape, 0) >> width_bits)
    within = iota(shape, 0) < 3 * width
    collect = jnp.concatenate(
        [(within & (away >= first) & (away < first + 3)).astype(jnp.bfloat16) for first in (0, 9, 18)], axis=0
    )

    def panel_vectors(number):
        got = got_ref[pl.ds(number * block_devices, block_devices), 0 : width // EXTRA].astype(jnp.float32)
        vectors = got.reshape(block, vec_count).astype(jnp.bfloat16)
        return mm(eye, vectors, dims=((1,), (1,))).astype(jnp.bfloat16)

    def panel_left(number):
        tail = got_ref[pl.ds(number * block_devices, block_devices), width // EXTRA].astype(jnp.float32)
        points = [jnp.where(keep, jnp.broadcast_to(tail[d, EXTRA - 1 : EXTRA], keep.shape), 0.0) for d in range(block_devices)]
        points = jnp.concatenate(points, axis=0)
        high, low = split2(points * points)
        left = mm(jnp.concatenate([points.astype(jnp.bfloat16), high, low], axis=1), collect) + ones
        left_ref[...] = left.astype(jnp.bfloat16)

    def fill(at, count, right, lane):
        dist = mm(left_ref[pl.ds(at, count), :], right)
        lanes = right.shape[1]
        kre_ref[pl.ds(at, count), lane : lane + lanes], kim_ref[pl.ds(at, count), lane : lane + lanes] = evaluate(dist)

    def sample(vectors, lane, lanes):
        both = [mm(vectors, k[:, lane : lane + lanes]) for k in (kre_ref, kim_ref)]
        return jnp.concatenate(both, axis=0)

    group_start = (leaf // group_leaves) * group_devices
    extra = got_ref[pl.ds(group_start, group_devices), width // EXTRA].astype(jnp.float32)
    extra = extra.reshape(group_devices * EXTRA, LANES).astype(jnp.bfloat16)
    shape = (7 * 16, group_devices * EXTRA)
    at = iota(shape, 0)
    line = at >> 4
    place = jnp.where(line < 3, line, jnp.where(line == 3, EXTRA, jnp.where(line == 4, EXTRA - 1, line)))
    source = ((at & 7) * 2 + ((at >> 3) & 1)) * (cols * EXTRA) + place
    picked = mm((iota(shape, 1) == source).astype(jnp.bfloat16), extra)
    even = [picked[r * 16 : r * 16 + 8] for r in range(7)]
    odd = [picked[r * 16 + 8 : r * 16 + 16] for r in range(7)]
    even_s = [swap_halves(v) for v in even]
    odd_s = [swap_halves(v) for v in odd]
    coords = [
        jnp.where(low8, even[0] + even_s[0] + even[1], odd[0] + odd_s[0] + odd_s[1]),
        jnp.where(low8, even_s[1] + (even[2] + even_s[2]), odd[1] + (odd[2] + odd_s[2])),
        jnp.where(low8, even[3] + even_s[3] + even_s[4], odd[3] + odd_s[3] + odd[4]),
    ]
    lists = [
        jnp.where(low8, even[5], even_s[5]).astype(jnp.int32),
        jnp.where(low8, even_s[5], even[5]).astype(jnp.int32),
        jnp.where(low8, even[6], even_s[6]).astype(jnp.int32),
        jnp.where(low8, even_s[6], even[6]).astype(jnp.int32),
    ]

    def own_row(x):
        return jnp.sum(jnp.where(mine, x, jnp.zeros_like(x)), axis=0, keepdims=True)

    siblings = []
    own_lists = [own_row(lists[0])]
    stacked = coords
    for level in range(1, levels):
        own = [take_lanes(v, lists[level - 1]) for v in stacked]
        step = 2 ** (level - 1)
        upper = (sub8 & step) != 0
        other = [jnp.where(upper, pltpu.roll(v, step, axis=0), pltpu.roll(v, SUB - step, axis=0)) for v in own]
        siblings.append([own_row(v) for v in other])
        stacked = [jnp.where(low8 == upper, b, a) for a, b in zip(own, other)]
        own_lists.append(own_row(lists[level]))
    low1 = iota((1, LANES), 1) < half
    tiles = [[own_row(v) for v in coords]]
    tiles.append([jnp.where(low1, a, b) for a, b in zip(siblings[0], siblings[1])])
    tiles.append(siblings[2])
    chunk = min(LANES, block)
    panel_left(0)
    right_own = right_side([own_points[c : c + 1] for c in range(3)])
    pieces = list(range(0, block, 16)) if single else []

    def own_pieces(count):
        for unused in range(min(count, len(pieces))):
            fill(pieces.pop(0), 16, right_own, tree_lanes)

    vectors = panel_vectors(0)
    right_tree = jnp.concatenate([right_side(t) for t in tiles], axis=1)

    for at in range(0, block, chunk):
        fill(at, chunk, right_tree, 0)
    samples_ref[:, 0:tree_lanes] = sample(vectors, 0, tree_lanes)
    if not single:
        for at in range(0, block, chunk):
            fill(at, chunk, right_own, tree_lanes)
        samples_ref[:, tree_lanes:] = sample(vectors, tree_lanes, own_rows)

        def more(number, unused):
            panel_left(number)
            for at in range(0, block, chunk):
                fill(at, chunk, right_tree, 0)
                fill(at, chunk, right_own, tree_lanes)
            samples_ref[...] += sample(panel_vectors(number), 0, tree_lanes + own_rows)
            return unused

        lax.fori_loop(1, devices // block_devices, more, 0)

    full = (2 * vec_count, LANES)
    low = iota(full, 1) < half
    pair0 = samples_ref[:, 0:LANES]
    pair0_s = swap_halves(pair0)
    pair12 = samples_ref[:, LANES : 2 * LANES]
    pair12_s = swap_halves(pair12)
    pair3 = samples_ref[:, 2 * LANES : 3 * LANES]

    def is_upper(level, shape):
        return (jnp.full(shape, member, jnp.int32) & 2**level) != 0

    upper0 = is_upper(0, full)
    stacks = [pair0]
    skels = [jnp.where(upper0 == low, pair0_s, pair0)]
    for level in range(levels):
        picked = take_lanes(stacks[level], jnp.broadcast_to(own_lists[level], full))
        skels.append(picked)
        own_pieces(STAGE_PIECES)
        if level + 1 < levels:
            up = is_upper(level + 1, full)
            if level == 0:
                other = jnp.where(up, pair12, pair12_s)
            elif level == 1:
                other = jnp.where(up, pair12_s, pair12)
            else:
                other = pair3
            stacks.append(jnp.where(low == up, other, picked))

    two = [jnp.where(low, skels[0], skels[1]).T, jnp.where(low, skels[2], skels[3]).T, skels[4].T]
    row_form = [two[0][0:half], two[0][half:], two[1][0:half], two[1][half:], two[2][0:half]]
    top_ref[0] = row_form[4]
    copies = []

    def send(source, target):
        copies.append(pltpu.make_async_copy(source, target, sems.at[len(copies)]))
        copies[-1].start()

    send(top_ref, top_out)
    row_form = [split2(v) for v in row_form]

    stacks = [split2(v) for v in stacks]
    square = (half, LANES)
    low64 = iota(square, 1) < half
    right_maps = [mm_split(row_form[level + 1], stacks[level]) for level in range(levels)]
    gram = mm_split(row_form[0], stacks[0])
    grams = [jnp.where(is_upper(0, square) == low64, swap_halves(gram), gram)]
    for level in range(levels):
        grams.append(take_lanes(right_maps[level], jnp.broadcast_to(own_lists[level], square)))
    pairs = []
    scales = []
    diagonal = iota(square, 0) == (iota(square, 1) & (half - 1))
    for a, b in ((0, 1), (2, 3), (4, 4)):
        gram = jnp.where(low64, grams[a], grams[b])
        trace = jnp.sum(jnp.where(diagonal, gram, 0.0), axis=0, keepdims=True)
        first = jnp.sum(jnp.where(low1, trace, 0.0), axis=1, keepdims=True)
        second = jnp.sum(jnp.where(low1, 0.0, trace), axis=1, keepdims=True)
        trace = jnp.where(low1, first, second)
        ridge = RIDGE * (2 * vec_count) * (trace * (1.0 / (half * 2 * vec_count)) + EPSILON)
        scales.append(RIDGE / ridge)
        gram = gram * scales[-1] + jnp.where(diagonal, RIDGE, 0.0)
        pairs.append([gram[r * SUB : (r + 1) * SUB] for r in range(half // SUB)])

    right_maps = [split2(v) for v in right_maps]
    where_in_half = lane8 & (half - 1)
    half_base = lane8 - where_in_half
    blocks = half // SUB

    def spread_row(x, row):
        return jnp.broadcast_to(x[row : row + 1], (SUB, LANES))

    def total_of(terms):
        while len(terms) > 1:
            terms = [x + y for x, y in zip(terms[::2], terms[1::2])]
        return terms[0]

    zero8 = jnp.zeros((SUB, LANES), jnp.float32)
    zero16 = jnp.zeros((2 * SUB, LANES), jnp.bfloat16)
    for turn in range(blocks):
        first = turn * SUB
        ahead = turn + 1 if turn + 1 < blocks else None
        within_turn = (where_in_half >> 3) == turn
        diagonals = [[take_lanes(a[turn], half_base + (first + j)) for j in range(SUB)] for a in pairs]
        if ahead is not None:
            nexts = [[take_lanes(a[ahead], half_base + (first + j)) for j in range(SUB)] for a in pairs]
        lines = [a[turn] for a in pairs]
        for s in range(SUB):
            own_pieces(TURN_PIECES[turn] if s % 2 == 0 else 0)
            here = where_in_half == first + s
            unit = jnp.where(sub8 == s, 1.0, 0.0)
            pivots = [spread_row(columns[s], s) for columns in diagonals]
            inverses = 1.0 / jnp.where(sub8 == 0, pivots[0], jnp.where(sub8 == 1, pivots[1], pivots[2]))
            for n in range(len(pairs)):
                columns = diagonals[n]
                inverse = spread_row(inverses, n)
                column = (columns[s] - unit) * inverse
                line = jnp.where(here, 1.0, spread_row(lines[n], s))
                lines[n] = jnp.where(here, unit, lines[n]) - column * line
                for j in range(s + 1, SUB):
                    columns[j] = columns[j] - column * spread_row(columns[j], s)
        if turn == LEAF_TURN:
            own_pieces(block)
            own_samples = sample(vectors, tree_lanes, own_rows) if single else samples_ref[:, tree_lanes:]
            right_leaf = split2(mm_split(row_form[0], split2(own_samples)))
        for n, a in enumerate(pairs):
            line = lines[n]
            cleared = [jnp.where(within_turn, 0.0, v) for v in a]
            others = [b for b in range(blocks) if b not in (turn, ahead)]
            if ahead is not None:
                a[ahead] = cleared[ahead] - total_of([nexts[n][j] * spread_row(line, j) for j in range(SUB)])

            def placed(part):
                pads = [zero16] * blocks
                both = [part, zero8] if turn % 2 == 0 else [zero8, part]
                for side, chosen in ((0, low8), (1, ~low8)):
                    pads[side * blocks // 2 + turn // 2] = jnp.concatenate(
                        [jnp.where(chosen, v, 0.0) for v in both], axis=0
                    ).astype(jnp.bfloat16)
                return jnp.concatenate(pads, axis=0)

            high = line.astype(jnp.bfloat16).astype(jnp.float32)
            right = placed(high), placed(line - high)
            padded = others + [turn] * (len(others) % 2)
            product = mm_split(split2(jnp.concatenate([a[b] for b in padded], axis=0)), right)
            for number, b in enumerate(others):
                a[b] = cleared[b] - product[number * SUB : (number + 1) * SUB]
            a[turn] = line

    inverses = []
    for a, scale in zip(pairs, scales):
        both = jnp.concatenate(a, axis=0) * scale
        inverses.append(split2(jnp.concatenate([jnp.where(low64, both, 0.0), jnp.where(low64, 0.0, both)], axis=0)))
    def times(pair, first, last, parts):
        left = [v[first:last] for v in pair]
        return mm_split(left, [jnp.concatenate(p, axis=0) if len(p) > 1 else p[0] for p in zip(*parts)])

    zero = [jnp.zeros((half, LANES), jnp.bfloat16)] * 2
    wide = [jnp.zeros((half, own_rows), jnp.bfloat16)] * 2
    result = times(inverses[1], 0, LANES, (right_maps[1], right_maps[2]))
    maps_ref[0, 1] = result[0:half]
    maps_ref[0, 2] = result[half:]
    maps_ref[0, 3] = times(inverses[2], 0, half, (right_maps[3], zero))
    send(maps_ref.at[:, 1:], maps_out.at[:, 1:])
    interp_ref[...] = times(inverses[0], 0, half, (right_leaf, wide))
    send(interp_ref, interp_out)
    maps_ref[0, 0] = times(inverses[0], half, LANES, (zero, right_maps[0]))
    send(maps_ref.at[:, 0:1], maps_out.at[:, 0:1])
    for copy in copies:
        copy.wait()


def body(row_points, panel_points, test_vectors, leaf_skeleton, node_skeleton):
    devices = lax.axis_size("rows") * lax.axis_size("cols")
    vec_count, width = test_vectors.shape
    rows_here = row_points.shape[1]
    levels, skel = node_skeleton.shape[1:]
    packed, kept = pl.pallas_call(
        pack_kernel,
        out_shape=(
            pltpu.VMEM((devices, width // EXTRA + 1, EXTRA, vec_count), jnp.bfloat16),
            pltpu.VMEM(row_points.shape, jnp.float32),
        ),
        in_specs=[VMEM] * 5,
        out_specs=(VMEM, VMEM),
        scratch_shapes=[pltpu.VMEM((SUB, LANES), jnp.float32)],
    )(row_points, panel_points, test_vectors.T, leaf_skeleton, node_skeleton)
    got = lax.all_to_all(packed, ("rows", "cols"), 0, 0, tiled=True)
    own_rows = rows_here // lax.axis_size("cols")
    lanes = 3 * LANES + own_rows
    block = min(devices, 2**levels * lax.axis_size("cols")) * width
    outs = (
        jax.ShapeDtypeStruct((skel, own_rows), jnp.float32),
        jax.ShapeDtypeStruct((1, levels, skel, 2 * skel), jnp.float32),
        jax.ShapeDtypeStruct((1, skel, 2 * vec_count), jnp.float32),
    )
    return pl.pallas_call(
        functools.partial(main_kernel, levels),
        out_shape=outs,
        in_specs=[VMEM] * 2,
        out_specs=tuple(pl.BlockSpec(memory_space=pl.ANY) for out in outs),
        scratch_shapes=[pltpu.VMEM(out.shape, out.dtype) for out in outs]
        + [
            pltpu.VMEM((block, LANES), jnp.bfloat16),
            pltpu.VMEM((block, lanes), jnp.bfloat16),
            pltpu.VMEM((block, lanes), jnp.bfloat16),
            pltpu.VMEM((2 * vec_count, lanes), jnp.float32),
            pltpu.SemaphoreType.DMA((4,)),
        ],
    )(pltpu.with_memory_space_constraint(got, pltpu.VMEM), pltpu.with_memory_space_constraint(kept, pltpu.VMEM))


def solution(mesh):
    placed = (
        P(None, "rows"),
        P(None, ("rows", "cols")),
        P(None, ("rows", "cols")),
        P("rows", None),
        P("rows", None, None),
    )
    return jax.shard_map(
        body,
        mesh=mesh,
        in_specs=placed,
        out_specs=(P(None, ("rows", "cols")), P("rows", None, None, None), P("rows", None, None)),
        check_vma=False,
    )
```

```python
import functools
import math

import jax
import jax.numpy as jnp
import numpy as np
from jax import lax
from jax.experimental import pallas as pl
from jax.experimental.pallas import tpu as pltpu
from jax.sharding import PartitionSpec as P

KAPPA = 40.0
SMOOTH = 0.05
RIDGE = 0.1
EPSILON = 1e-05

LANES = 128
SUB = 8
EXTRA = 4
VMEM = pl.BlockSpec(memory_space=pltpu.VMEM)

TURNS = KAPPA / (2 * math.pi)
SIN_POLY = (4.442867902871973, -7.30744341774541, 3.594788055359915, -0.7843739844598376)
COS_POLY = (1.4142134965650128, -6.978850988238946, 5.739461170681512, -1.8835629873012505, 0.31069819181076774)


def bf16_parts(value):
    parts = []
    for unused in range(3):
        parts.append(float(np.float32(value).astype(jnp.bfloat16)))
        value -= parts[-1]
    return parts


SCALE_PARTS = bf16_parts(TURNS * TURNS)


def iota(shape, dim):
    return lax.broadcasted_iota(jnp.int32, shape, dim)


def take_lanes(x, index):
    return jnp.take_along_axis(x, index, axis=1)


def swap_halves(x):
    return pltpu.roll(x, LANES // 2, axis=1)


def mm(a, b, dims=((1,), (0,)), precision=None):
    return lax.dot_general(a, b, (dims, ((), ())), precision=precision, preferred_element_type=jnp.float32)


def split2(x):
    high = x.astype(jnp.bfloat16)
    return high, (x - high.astype(jnp.float32)).astype(jnp.bfloat16)


def mm_split(a, b):
    rows, lanes = a[0].shape[0], b[0].shape[1]
    out = mm(jnp.concatenate(a, axis=0), jnp.concatenate(b, axis=1))
    return out[:rows, :lanes] + (out[:rows, lanes:] + out[rows:, :lanes])


def split3(x):
    high = x.astype(jnp.bfloat16).astype(jnp.float32)
    rest = x - high
    mid = rest.astype(jnp.bfloat16).astype(jnp.float32)
    return high, mid, rest - mid


def pack_kernel(rows_ref, points_ref, vectors_ref, leaf_ref, node_ref, out_ref, kept_ref, stage):
    kept_ref[...] = rows_ref[...]
    width = vectors_ref.shape[0]
    half = LANES // 2
    low = iota((1, LANES), 1) < half
    stage[...] = jnp.zeros_like(stage)
    stage[0:1, 0:half] = leaf_ref[...].astype(jnp.float32)
    stage[1:5, 0:half] = node_ref[0].astype(jnp.float32)
    stage[5:8, 0:width] = points_ref[...].astype(jnp.float32)
    s = stage[...]
    index = s[0:1]
    index = (index + swap_halves(jnp.broadcast_to(index, (SUB, LANES)))[0:1]).astype(jnp.int32)
    index = jnp.broadcast_to(index, (SUB, LANES))
    found = jnp.zeros((SUB, LANES), jnp.float32)
    for tile in range(rows_ref.shape[1] // LANES):
        part = rows_ref[:, tile * LANES : (tile + 1) * LANES]
        part = jnp.concatenate([part, jnp.zeros((SUB - part.shape[0], LANES), jnp.float32)], axis=0)
        picked = take_lanes(part, index & (LANES - 1))
        found = jnp.where(index // LANES == tile, picked, found)
    high, mid, tail = split3(found)
    swapped = swap_halves(s)
    points = s[5:6] + pltpu.roll(s, width, axis=1)[6:7] + pltpu.roll(s, 2 * width, axis=1)[7:8]
    halves = (
        [
            jnp.where(low, high[0:1], mid[0:1]),
            jnp.where(low, tail[0:1], high[1:2]),
            jnp.where(low, mid[1:2], tail[1:2]),
        ],
        [
            jnp.where(low, high[2:3], mid[2:3]),
            jnp.where(low, s[1:2], swapped[2:3]),
            jnp.where(low, s[3:4], swapped[4:5]),
        ],
    )
    column = lax.axis_index("cols")
    lines = [jnp.where(column == 0, a, b) for a, b in zip(*halves)]
    lines.append(jnp.where(low, points, tail[2:3]))
    block = jnp.concatenate([vectors_ref[...].astype(jnp.float32)] + lines, axis=0).astype(jnp.bfloat16)

    block = block.reshape(out_ref.shape[1:])

    def put(device, unused):
        out_ref[device] = block
        return unused

    lax.fori_loop(0, out_ref.shape[0], put, 0, unroll=16)


STAGE_PIECES = 8
TURN_PIECES = (0, 0, 0, 0, 0, 0, 0, 0)
LEAF_TURN = 3


def evaluate(dist):
    inverse = lax.rsqrt(dist)
    turns = dist * inverse
    f = turns - jnp.round(turns)
    u = f * f
    scale = math.sqrt(TURNS)
    sine = SIN_POLY[-1] * scale
    cosine = COS_POLY[-1] * scale
    for value in SIN_POLY[-2::-1]:
        sine = sine * u + value * scale
    for value in COS_POLY[-2::-1]:
        cosine = cosine * u + value * scale
    sine = sine * f
    real = (TURNS - sine * sine) * inverse
    imag = (sine * cosine) * inverse
    return real.astype(jnp.bfloat16), imag.astype(jnp.bfloat16)


def main_kernel(levels, got_ref, rows_ref, interp_out, maps_out, top_out, interp_ref, maps_ref, top_ref, left_ref, kre_ref, kim_ref, samples_ref, sems):
    half = LANES // 2
    leaf = lax.axis_index("rows")
    column = lax.axis_index("cols")
    cols = lax.axis_size("cols")
    group_leaves = 2**levels
    group_devices = group_leaves * cols
    devices = got_ref.shape[0]
    width = (got_ref.shape[1] - 1) * EXTRA
    width_bits = width.bit_length() - 1
    lane8 = iota((SUB, LANES), 1)
    sub8 = iota((SUB, LANES), 0)
    low8 = lane8 < half
    member = leaf & (group_leaves - 1)
    mine = sub8 == member >> 1

    tree_lanes = 3 * LANES
    own_rows = rows_ref.shape[1] // cols
    start = pl.multiple_of(column * own_rows, LANES)
    own_points = rows_ref[:, pl.ds(start, own_rows)]

    def right_side(points):
        lanes = points[0].shape[1]
        lines = []
        norm = jnp.full((1, lanes), SMOOTH * SMOOTH, jnp.float32)
        for x in points:
            norm = norm + x * x
            lines += split3(x * (-2 * TURNS * TURNS))
        for repeat in range(6):
            lines += [jnp.full((1, lanes), v, jnp.float32) for v in SCALE_PARTS]
        lines += split3(norm * (TURNS * TURNS))
        lines.append(jnp.zeros((LANES - len(lines), lanes), jnp.float32))
        return jnp.concatenate(lines, axis=0).astype(jnp.bfloat16)

    block_devices = min(devices, group_devices)
    single = block_devices == devices
    block = block_devices * width
    vec_count = got_ref.shape[-1]
    eye = (iota((vec_count, vec_count), 0) == iota((vec_count, vec_count), 1)).astype(jnp.bfloat16)
    shape = (width, LANES)
    lane_of = iota(shape, 1)
    keep = (((lane_of ^ iota(shape, 0)) & (width - 1)) == 0) & (lane_of < 3 * width)
    ones = ((iota((1, LANES), 1) >= 27) & (iota((1, LANES), 1) < 30)).astype(jnp.float32)
    shape = (LANES, LANES)
    away = iota(shape, 1) - 3 * (iota(shape, 0) >> width_bits)
    within = iota(shape, 0) < 3 * width
    collect = jnp.concatenate(
        [(within & (away >= first) & (away < first + 3)).astype(jnp.bfloat16) for first in (0, 9, 18)], axis=0
    )

    def panel_vectors(number):
        got = got_ref[pl.ds(number * block_devices, block_devices), 0 : width // EXTRA].astype(jnp.float32)
        vectors = got.reshape(block, vec_count).astype(jnp.bfloat16)
        return mm(eye, vectors, dims=((1,), (1,))).astype(jnp.bfloat16)

    def panel_left(number):
        tail = got_ref[pl.ds(number * block_devices, block_devices), width // EXTRA].astype(jnp.float32)
        points = [jnp.where(keep, jnp.broadcast_to(tail[d, EXTRA - 1 : EXTRA], keep.shape), 0.0) for d in range(block_devices)]
        points = jnp.concatenate(points, axis=0)
        high, low = split2(points * points)
        left = mm(jnp.concatenate([points.astype(jnp.bfloat16), high, low], axis=1), collect) + ones
        left_ref[...] = left.astype(jnp.bfloat16)

    def fill(at, count, right, lane):
        dist = mm(left_ref[pl.ds(at, count), :], right)
        lanes = right.shape[1]
        kre_ref[pl.ds(at, count), lane : lane + lanes], kim_ref[pl.ds(at, count), lane : lane + lanes] = evaluate(dist)

    def sample(vectors, lane, lanes):
        both = [mm(vectors, k[:, lane : lane + lanes]) for k in (kre_ref, kim_ref)]
        return jnp.concatenate(both, axis=0)

    group_start = (leaf // group_leaves) * group_devices
    extra = got_ref[pl.ds(group_start, group_devices), width // EXTRA].astype(jnp.float32)
    extra = extra.reshape(group_devices * EXTRA, LANES).astype(jnp.bfloat16)
    shape = (7 * 16, group_devices * EXTRA)
    at = iota(shape, 0)
    line = at >> 4
    place = jnp.where(line < 3, line, jnp.where(line == 3, EXTRA, jnp.where(line == 4, EXTRA - 1, line)))
    source = ((at & 7) * 2 + ((at >> 3) & 1)) * (cols * EXTRA) + place
    picked = mm((iota(shape, 1) == source).astype(jnp.bfloat16), extra)
    even = [picked[r * 16 : r * 16 + 8] for r in range(7)]
    odd = [picked[r * 16 + 8 : r * 16 + 16] for r in range(7)]
    even_s = [swap_halves(v) for v in even]
    odd_s = [swap_halves(v) for v in odd]
    coords = [
        jnp.where(low8, even[0] + even_s[0] + even[1], odd[0] + odd_s[0] + odd_s[1]),
        jnp.where(low8, even_s[1] + (even[2] + even_s[2]), odd[1] + (odd[2] + odd_s[2])),
        jnp.where(low8, even[3] + even_s[3] + even_s[4], odd[3] + odd_s[3] + odd[4]),
    ]
    lists = [
        jnp.where(low8, even[5], even_s[5]).astype(jnp.int32),
        jnp.where(low8, even_s[5], even[5]).astype(jnp.int32),
        jnp.where(low8, even[6], even_s[6]).astype(jnp.int32),
        jnp.where(low8, even_s[6], even[6]).astype(jnp.int32),
    ]

    def own_row(x):
        return jnp.sum(jnp.where(mine, x, jnp.zeros_like(x)), axis=0, keepdims=True)

    siblings = []
    own_lists = [own_row(lists[0])]
    stacked = coords
    for level in range(1, levels):
        own = [take_lanes(v, lists[level - 1]) for v in stacked]
        step = 2 ** (level - 1)
        upper = (sub8 & step) != 0
        other = [jnp.where(upper, pltpu.roll(v, step, axis=0), pltpu.roll(v, SUB - step, axis=0)) for v in own]
        siblings.append([own_row(v) for v in other])
        stacked = [jnp.where(low8 == upper, b, a) for a, b in zip(own, other)]
        own_lists.append(own_row(lists[level]))
    low1 = iota((1, LANES), 1) < half
    tiles = [[own_row(v) for v in coords]]
    tiles.append([jnp.where(low1, a, b) for a, b in zip(siblings[0], siblings[1])])
    tiles.append(siblings[2])
    chunk = min(LANES, block)
    panel_left(0)
    right_own = right_side([own_points[c : c + 1] for c in range(3)])
    pieces = list(range(0, block, 16)) if single else []

    def own_pieces(count):
        for unused in range(min(count, len(pieces))):
            fill(pieces.pop(0), 16, right_own, tree_lanes)

    vectors = panel_vectors(0)
    right_tree = jnp.concatenate([right_side(t) for t in tiles], axis=1)

    for at in range(0, block, chunk):
        fill(at, chunk, right_tree, 0)
    samples_ref[:, 0:tree_lanes] = sample(vectors, 0, tree_lanes)
    if not single:
        for at in range(0, block, chunk):
            fill(at, chunk, right_own, tree_lanes)
        samples_ref[:, tree_lanes:] = sample(vectors, tree_lanes, own_rows)

        def more(number, unused):
            panel_left(number)
            for at in range(0, block, chunk):
                fill(at, chunk, right_tree, 0)
                fill(at, chunk, right_own, tree_lanes)
            samples_ref[...] += sample(panel_vectors(number), 0, tree_lanes + own_rows)
            return unused

        lax.fori_loop(1, devices // block_devices, more, 0)

    full = (2 * vec_count, LANES)
    low = iota(full, 1) < half
    pair0 = samples_ref[:, 0:LANES]
    pair0_s = swap_halves(pair0)
    pair12 = samples_ref[:, LANES : 2 * LANES]
    pair12_s = swap_halves(pair12)
    pair3 = samples_ref[:, 2 * LANES : 3 * LANES]

    def is_upper(level, shape):
        return (jnp.full(shape, member, jnp.int32) & 2**level) != 0

    upper0 = is_upper(0, full)
    stacks = [pair0]
    skels = [jnp.where(upper0 == low, pair0_s, pair0)]
    for level in range(levels):
        picked = take_lanes(stacks[level], jnp.broadcast_to(own_lists[level], full))
        skels.append(picked)
        own_pieces(STAGE_PIECES)
        if level + 1 < levels:
            up = is_upper(level + 1, full)
            if level == 0:
                other = jnp.where(up, pair12, pair12_s)
            elif level == 1:
                other = jnp.where(up, pair12_s, pair12)
            else:
                other = pair3
            stacks.append(jnp.where(low == up, other, picked))

    two = [jnp.where(low, skels[0], skels[1]).T, jnp.where(low, skels[2], skels[3]).T, skels[4].T]
    row_form = [two[0][0:half], two[0][half:], two[1][0:half], two[1][half:], two[2][0:half]]
    top_ref[0] = row_form[4]
    copies = []

    def send(source, target):
        copies.append(pltpu.make_async_copy(source, target, sems.at[len(copies)]))
        copies[-1].start()

    send(top_ref, top_out)
    row_form = [split2(v) for v in row_form]

    stacks = [split2(v) for v in stacks]
    square = (half, LANES)
    low64 = iota(square, 1) < half
    right_maps = [mm_split(row_form[level + 1], stacks[level]) for level in range(levels)]
    gram = mm_split(row_form[0], stacks[0])
    grams = [jnp.where(is_upper(0, square) == low64, swap_halves(gram), gram)]
    for level in range(levels):
        grams.append(take_lanes(right_maps[level], jnp.broadcast_to(own_lists[level], square)))
    pairs = []
    scales = []
    diagonal = iota(square, 0) == (iota(square, 1) & (half - 1))
    for a, b in ((0, 1), (2, 3), (4, 4)):
        gram = jnp.where(low64, grams[a], grams[b])
        trace = jnp.sum(jnp.where(diagonal, gram, 0.0), axis=0, keepdims=True)
        first = jnp.sum(jnp.where(low1, trace, 0.0), axis=1, keepdims=True)
        second = jnp.sum(jnp.where(low1, 0.0, trace), axis=1, keepdims=True)
        trace = jnp.where(low1, first, second)
        ridge = RIDGE * (2 * vec_count) * (trace * (1.0 / (half * 2 * vec_count)) + EPSILON)
        scales.append(RIDGE / ridge)
        gram = gram * scales[-1] + jnp.where(diagonal, RIDGE, 0.0)
        pairs.append([gram[r * SUB : (r + 1) * SUB] for r in range(half // SUB)])

    right_maps = [split2(v) for v in right_maps]
    where_in_half = lane8 & (half - 1)
    half_base = lane8 - where_in_half
    blocks = half // SUB

    def spread_row(x, row):
        return jnp.broadcast_to(x[row : row + 1], (SUB, LANES))

    def total_of(terms):
        while len(terms) > 1:
            terms = [x + y for x, y in zip(terms[::2], terms[1::2])]
        return terms[0]

    zero8 = jnp.zeros((SUB, LANES), jnp.float32)
    zero16 = jnp.zeros((2 * SUB, LANES), jnp.bfloat16)
    for turn in range(blocks):
        first = turn * SUB
        ahead = turn + 1 if turn + 1 < blocks else None
        within_turn = (where_in_half >> 3) == turn
        diagonals = [[take_lanes(a[turn], half_base + (first + j)) for j in range(SUB)] for a in pairs]
        if ahead is not None:
            nexts = [[take_lanes(a[ahead], half_base + (first + j)) for j in range(SUB)] for a in pairs]
        lines = [a[turn] for a in pairs]
        for s in range(SUB):
            own_pieces(TURN_PIECES[turn] if s % 2 == 0 else 0)
            here = where_in_half == first + s
            unit = jnp.where(sub8 == s, 1.0, 0.0)
            pivots = [spread_row(columns[s], s) for columns in diagonals]
            inverses = 1.0 / jnp.where(sub8 == 0, pivots[0], jnp.where(sub8 == 1, pivots[1], pivots[2]))
            for n in range(len(pairs)):
                columns = diagonals[n]
                inverse = spread_row(inverses, n)
                column = (columns[s] - unit) * inverse
                line = jnp.where(here, 1.0, spread_row(lines[n], s))
                lines[n] = jnp.where(here, unit, lines[n]) - column * line
                for j in range(s + 1, SUB):
                    columns[j] = columns[j] - column * spread_row(columns[j], s)
        if turn == LEAF_TURN:
            own_pieces(block)
            own_samples = sample(vectors, tree_lanes, own_rows) if single else samples_ref[:, tree_lanes:]
            right_leaf = split2(mm_split(row_form[0], split2(own_samples)))
        for n, a in enumerate(pairs):
            line = lines[n]
            cleared = [jnp.where(within_turn, 0.0, v) for v in a]
            others = [b for b in range(blocks) if b not in (turn, ahead)]
            if ahead is not None:
                a[ahead] = cleared[ahead] - total_of([nexts[n][j] * spread_row(line, j) for j in range(SUB)])

            def placed(part):
                pads = [zero16] * blocks
                both = [part, zero8] if turn % 2 == 0 else [zero8, part]
                for side, chosen in ((0, low8), (1, ~low8)):
                    pads[side * blocks // 2 + turn // 2] = jnp.concatenate(
                        [jnp.where(chosen, v, 0.0) for v in both], axis=0
                    ).astype(jnp.bfloat16)
                return jnp.concatenate(pads, axis=0)

            high = line.astype(jnp.bfloat16).astype(jnp.float32)
            right = placed(high), placed(line - high)
            padded = others + [turn] * (len(others) % 2)
            product = mm_split(split2(jnp.concatenate([a[b] for b in padded], axis=0)), right)
            for number, b in enumerate(others):
                a[b] = cleared[b] - product[number * SUB : (number + 1) * SUB]
            a[turn] = line

    inverses = []
    for a, scale in zip(pairs, scales):
        both = jnp.concatenate(a, axis=0) * scale
        inverses.append(split2(jnp.concatenate([jnp.where(low64, both, 0.0), jnp.where(low64, 0.0, both)], axis=0)))
    def times(pair, first, last, parts):
        left = [v[first:last] for v in pair]
        return mm_split(left, [jnp.concatenate(p, axis=0) if len(p) > 1 else p[0] for p in zip(*parts)])

    zero = [jnp.zeros((half, LANES), jnp.bfloat16)] * 2
    wide = [jnp.zeros((half, own_rows), jnp.bfloat16)] * 2
    result = times(inverses[1], 0, LANES, (right_maps[1], right_maps[2]))
    maps_ref[0, 1] = result[0:half]
    maps_ref[0, 2] = result[half:]
    maps_ref[0, 3] = times(inverses[2], 0, half, (right_maps[3], zero))
    send(maps_ref.at[:, 1:], maps_out.at[:, 1:])
    interp_ref[...] = times(inverses[0], 0, half, (right_leaf, wide))
    send(interp_ref, interp_out)
    maps_ref[0, 0] = times(inverses[0], half, LANES, (zero, right_maps[0]))
    send(maps_ref.at[:, 0:1], maps_out.at[:, 0:1])
    for copy in copies:
        copy.wait()


def body(row_points, panel_points, test_vectors, leaf_skeleton, node_skeleton):
    devices = lax.axis_size("rows") * lax.axis_size("cols")
    vec_count, width = test_vectors.shape
    rows_here = row_points.shape[1]
    levels, skel = node_skeleton.shape[1:]
    packed, kept = pl.pallas_call(
        pack_kernel,
        out_shape=(
            pltpu.VMEM((devices, width // EXTRA + 1, EXTRA, vec_count), jnp.bfloat16),
            pltpu.VMEM(row_points.shape, jnp.float32),
        ),
        in_specs=[VMEM] * 5,
        out_specs=(VMEM, VMEM),
        scratch_shapes=[pltpu.VMEM((SUB, LANES), jnp.float32)],
    )(row_points, panel_points, test_vectors.T, leaf_skeleton, node_skeleton)
    got = lax.all_to_all(packed, ("rows", "cols"), 0, 0, tiled=True)
    own_rows = rows_here // lax.axis_size("cols")
    lanes = 3 * LANES + own_rows
    block = min(devices, 2**levels * lax.axis_size("cols")) * width
    outs = (
        jax.ShapeDtypeStruct((skel, own_rows), jnp.float32),
        jax.ShapeDtypeStruct((1, levels, skel, 2 * skel), jnp.float32),
        jax.ShapeDtypeStruct((1, skel, 2 * vec_count), jnp.float32),
    )
    return pl.pallas_call(
        functools.partial(main_kernel, levels),
        out_shape=outs,
        in_specs=[VMEM] * 2,
        out_specs=tuple(pl.BlockSpec(memory_space=pl.ANY) for out in outs),
        scratch_shapes=[pltpu.VMEM(out.shape, out.dtype) for out in outs]
        + [
            pltpu.VMEM((block, LANES), jnp.bfloat16),
            pltpu.VMEM((block, lanes), jnp.bfloat16),
            pltpu.VMEM((block, lanes), jnp.bfloat16),
            pltpu.VMEM((2 * vec_count, lanes), jnp.float32),
            pltpu.SemaphoreType.DMA((4,)),
        ],
        compiler_params=pltpu.CompilerParams(),
    )(pltpu.with_memory_space_constraint(got, pltpu.VMEM), pltpu.with_memory_space_constraint(kept, pltpu.VMEM))


def solution(mesh):
    placed = (
        P(None, "rows"),
        P(None, ("rows", "cols")),
        P(None, ("rows", "cols")),
        P("rows", None),
        P("rows", None, None),
    )
    return jax.shard_map(
        body,
        mesh=mesh,
        in_specs=placed,
        out_specs=(P(None, ("rows", "cols")), P("rows", None, None, None), P("rows", None, None)),
        check_vma=False,
    )
```
